32 devices in a mesh: groups: 2 (over y), srv: 4 (over z), hid: 2 (over x), rep: 2 (over core).
Axes of the slice: x: 2, y: 2, z: 4, core: 2. Of those that a mesh axis runs over, the one named last changes fastest.
Arguments:
- layer_input: bfloat16 [2048, 4096], P(('groups', 'srv'), ('hid', 'rep')), parts along dimension 0, may hold values from -12 to 12
- query_weight: bfloat16 [4096, 4096], P('srv', ('hid', 'rep')), may hold values from -0.09375 to 0.09375
- key_weight: bfloat16 [4096, 1024], P('srv', ('hid', 'rep')), may hold values from -0.09375 to 0.09375
- value_weight: bfloat16 [4096, 1024], P('srv', ('hid', 'rep')), may hold values from -0.09375 to 0.09375
- out_grad: bfloat16 [2048, 4096], P(('groups', 'srv'), ('hid', 'rep')), parts along dimension 0, may hold values from -6 to 6
- doc_ids: int32 [2048], P('groups'), parts along dimension 0, may hold values from 0 to 7, never falling along the last dimension, each value on 1 to 512 neighbouring positions
Outputs:
- input_grad: bfloat16 [2048, 4096], P(('groups', 'srv'), ('hid', 'rep')), parts along dimension 0
- query_weight_grad: float32 [8192, 4096], P(('groups', 'srv'), ('hid', 'rep')), parts along dimension 0
- key_weight_grad: float32 [8192, 1024], P(('groups', 'srv'), ('hid', 'rep')), parts along dimension 0
- value_weight_grad: float32 [8192, 1024], P(('groups', 'srv'), ('hid', 'rep')), parts along dimension 0
The draws below stay inside these ranges and needn't reach their ends.
There are 2 independent parts, one for each index of `groups`. The reference program is written for one: setup_inputs(seed, part) draws one part's arguments, and reference() takes and returns one part's arrays. A program takes and returns all parts, laid end to end along the dimension named above; an argument that names none is the same for every part. Nothing has to cross between parts.
Inputs may be any that keep to these rules, and one draw needn't show every extreme that they name: `doc_ids`: document numbers never fall along the tokens; every document holds at most 512 tokens and one holds exactly 512.
All inputs are finite; a program needn't handle non-finite values.
Results may differ from the reference program's by a relative error of at most 0.011.
Values may be sent and summed in bfloat16 or wider, within the bound.
A program may use at most 64 MiB of HBM per device.

```python
import math
import jax
import jax.numpy as jnp
import numpy as np
from jax import lax

D = 4096
HQ = 32
HK = 8
DH = 128
DOCS = 8
TOKENS = 1024
MAXDOC = 512


def draw_layer_input(key, part):
    values_drawn = jax.random.normal(jax.random.fold_in(key, 11), (TOKENS, D), jnp.float32)
    values_drawn = jnp.clip(values_drawn, -6.0, 6.0)
    return values_drawn.astype(jnp.bfloat16)


def block_levels(rng, extent, cuts, smallest, largest):
    factor_of = 1.0
    for dim, shards_of in cuts:
        heights = jax.random.uniform(jax.random.fold_in(jax.random.fold_in(rng, 6), dim), (shards_of,), jnp.float32, smallest / len(cuts), largest / len(cuts))
        factor_of = factor_of * jnp.repeat(jnp.exp(heights), extent[dim] // shards_of).reshape((-1,) + (1,) * (len(extent) - 1 - dim))
    return factor_of


def length_profile(count, total, limit, skew):
    weights = [(1 << 20) // math.isqrt(rank ** skew) + 1 for rank in range(2, count + 1)]
    spare, holding = total - limit - (count - 1), [1] * (count - 1)
    while spare > 0:
        movable = [i for i in range(count - 1) if holding[i] < limit]
        whole, remaining = sum([weights[i] for i in movable]), spare
        for i in movable:
            more = min(limit - holding[i], max(1, remaining * weights[i] // whole), spare)
            holding[i] = holding[i] + more
            spare = spare - more
    return np.array([limit] + holding)


def uneven_parts(own_key, number_of, total, limit, skew):
    if number_of == 2:
        one = jax.random.randint(own_key, (), max(1, total - limit), min(limit, total - 1) + 1)
        return jnp.stack([one, total - one])
    sizes = jnp.asarray(length_profile(number_of, total, limit, skew), jnp.int32)
    pairs = (number_of - 1) // 2
    giver, sink = sizes[1:1 + 2 * pairs:2], sizes[2:2 + 2 * pairs:2]
    margin = jnp.minimum(giver - 1, limit - sink)
    shifted = jax.random.randint(jax.random.fold_in(own_key, 1), (pairs,), 0, 1 << 20) % (margin + 1)
    sizes = sizes.at[1:1 + 2 * pairs:2].set(giver - shifted).at[2:2 + 2 * pairs:2].set(sink + shifted)
    return sizes[jax.random.permutation(jax.random.fold_in(own_key, 2), number_of)]


def centred(key, extent, deviation, bound, pieces=(), kind=jnp.bfloat16):
    array = jax.random.normal(key, extent, jnp.float32) * deviation
    if len(pieces) > 0:
        array = block_levels(key, extent, pieces, -0.22, 0.18) * array
    return jnp.clip(array, min=-bound, max=bound).astype(kind)


def setup_inputs(seed: int = 0, part: int = 0) -> dict:
    keys = jax.random.split(jax.random.key(seed), 7)
    own_keys = jax.random.split(jax.random.fold_in(keys[6], part), 7)
    layer_input = draw_layer_input(jax.random.fold_in(jax.random.fold_in(keys[6], part), 71), part)
    query_weight = centred(keys[1], (D, HQ * DH), D ** -0.5, 0.09375, ((0, 4), (1, 4)))
    key_weight = centred(keys[2], (D, HK * DH), D ** -0.5, 0.09375, ((0, 4), (1, 4)))
    value_weight = centred(keys[3], (D, HK * DH), D ** -0.5, 0.09375, ((0, 4), (1, 4)))
    out_grad = centred(own_keys[4], (TOKENS, HQ * DH), 1.0, 6.0, ((0, 4), (1, 4)))
    doc_ids = jnp.searchsorted(jnp.cumsum(uneven_parts(own_keys[5], DOCS, TOKENS, MAXDOC, 2)), jnp.arange(TOKENS), side="right").astype(jnp.int32)
    return dict(layer_input=layer_input, query_weight=query_weight, key_weight=key_weight, value_weight=value_weight, out_grad=out_grad, doc_ids=doc_ids)


NEGATIVE = -1e30


def reference(layer_input, query_weight, key_weight, value_weight, out_grad, doc_ids):
    total_rows = layer_input.shape[0]
    group_size = HQ // HK
    factor_scale = DH ** -0.5
    queries = jnp.dot(layer_input, query_weight, preferred_element_type=jnp.float32).astype(jnp.bfloat16).reshape(total_rows, HQ, DH)
    keys_all = jnp.dot(layer_input, key_weight, preferred_element_type=jnp.float32).astype(jnp.bfloat16).reshape(total_rows, HK, DH)
    values_all = jnp.dot(layer_input, value_weight, preferred_element_type=jnp.float32).astype(jnp.bfloat16).reshape(total_rows, HK, DH)
    cotangent = out_grad.reshape(total_rows, HQ, DH)
    positions = jnp.arange(total_rows, dtype=jnp.int32)
    allowed = (doc_ids[None, :] == doc_ids[:, None]) & (positions[None, :] <= positions[:, None])

    def one_head(head_id):
        pair_id = head_id // group_size
        query_rows = lax.dynamic_index_in_dim(queries, head_id, 1, keepdims=False)
        key_rows = lax.dynamic_index_in_dim(keys_all, pair_id, 1, keepdims=False)
        value_rows = lax.dynamic_index_in_dim(values_all, pair_id, 1, keepdims=False)
        grad_rows = lax.dynamic_index_in_dim(cotangent, head_id, 1, keepdims=False)
        logits = jnp.dot(query_rows, key_rows.T, preferred_element_type=jnp.float32) * factor_scale
        logits = jnp.where(allowed, logits, NEGATIVE)
        weights = jnp.where(allowed, jnp.exp(logits - jnp.max(logits, axis=1, keepdims=True)), 0.0)
        attention = weights / jnp.sum(weights, axis=1, keepdims=True)
        slopes = jnp.dot(grad_rows, value_rows.T, preferred_element_type=jnp.float32)
        inner_sum = jnp.sum(attention * slopes, axis=1, keepdims=True)
        score_grad = (attention * (slopes - inner_sum) * factor_scale).astype(jnp.bfloat16)
        value_grad = jnp.dot(attention.astype(jnp.bfloat16).T, grad_rows, preferred_element_type=jnp.float32)
        key_grad = jnp.dot(score_grad.T, query_rows, preferred_element_type=jnp.float32)
        query_grad = jnp.dot(score_grad, key_rows, preferred_element_type=jnp.float32)
        return query_grad, key_grad, value_grad

    query_grad, key_grad, value_grad = lax.map(one_head, jnp.arange(HQ, dtype=jnp.int32))
    query_grad = jnp.transpose(query_grad.astype(jnp.bfloat16), (1, 0, 2)).reshape(total_rows, HQ * DH)
    key_grad = jnp.sum(key_grad.reshape(HK, group_size, total_rows, DH), axis=1).astype(jnp.bfloat16)
    key_grad = jnp.transpose(key_grad, (1, 0, 2)).reshape(total_rows, HK * DH)
    value_grad = jnp.sum(value_grad.reshape(HK, group_size, total_rows, DH), axis=1).astype(jnp.bfloat16)
    value_grad = jnp.transpose(value_grad, (1, 0, 2)).reshape(total_rows, HK * DH)
    input_grad = jnp.dot(query_grad, query_weight.T, preferred_element_type=jnp.float32)
    input_grad = input_grad + jnp.dot(key_grad, key_weight.T, preferred_element_type=jnp.float32)
    input_grad = input_grad + jnp.dot(value_grad, value_weight.T, preferred_element_type=jnp.float32)
    query_weight_grad = jnp.dot(layer_input.T, query_grad, preferred_element_type=jnp.float32)
    key_weight_grad = jnp.dot(layer_input.T, key_grad, preferred_element_type=jnp.float32)
    value_weight_grad = jnp.dot(layer_input.T, value_grad, preferred_element_type=jnp.float32)
    return input_grad.astype(jnp.bfloat16), query_weight_grad, key_weight_grad, value_weight_grad
```

```python
import functools

import jax
import jax.numpy as jnp
from jax import lax
from jax.experimental import pallas as pl
from jax.experimental.pallas import tpu as pltpu
from jax.sharding import PartitionSpec as P

HQ = 32
HK = 8
DH = 128
BLOCK = 128


NEGATIVE = -1e30


def attend(queries, cotangent, keys_all, values_all, doc_ids, block_id, carried):
    row_count = queries.shape[0]
    factor_scale = queries.shape[-1] ** (-0.5)
    offsets = jnp.arange(row_count, dtype=jnp.int32)
    query_pos = block_id * row_count + offsets
    query_doc = lax.dynamic_slice_in_dim(doc_ids, block_id * row_count, row_count)
    doc_start = jnp.sum((doc_ids < query_doc[0]).astype(jnp.int32))
    lowest = doc_start // row_count
    highest = jnp.where(True, block_id + 1, lowest)

    def scores_at(key_block):
        key_rows = lax.dynamic_slice_in_dim(keys_all, key_block * row_count, row_count, 0)
        value_rows = lax.dynamic_slice_in_dim(values_all, key_block * row_count, row_count, 0)
        key_doc = lax.dynamic_slice_in_dim(doc_ids, key_block * row_count, row_count)
        key_pos = key_block * row_count + offsets
        allowed = (key_doc[None, :] == query_doc[:, None]) & (
            key_pos[None, :] <= query_pos[:, None]
        )
        logits = (
            jnp.einsum("qgnd,kgd->gnqk", queries, key_rows, preferred_element_type=jnp.float32)
            * factor_scale
        )
        logits = jnp.where(allowed, logits, NEGATIVE)
        slopes = jnp.einsum(
            "qgnd,kgd->gnqk", cotangent, value_rows, preferred_element_type=jnp.float32
        )
        return (key_rows, allowed, logits, slopes)

    def first_pass(key_block, loop_state):
        row_peak, row_total, row_inner = loop_state
        key_rows, allowed, logits, slopes = scores_at(key_block)
        new_peak = jnp.maximum(row_peak, jnp.max(logits, axis=-1))
        weights = jnp.where(allowed, jnp.exp(logits - new_peak[..., None]), 0.0)
        factor = jnp.exp(row_peak - new_peak)
        row_total = row_total * factor + jnp.sum(weights, axis=-1)
        row_inner = row_inner * factor + jnp.sum(weights * slopes, axis=-1)
        return (new_peak, row_total, row_inner)

    stat_shape = (queries.shape[1], queries.shape[2], row_count)
    initial = (
        jnp.full(stat_shape, NEGATIVE, jnp.float32),
        jnp.zeros(stat_shape, jnp.float32),
        jnp.zeros(stat_shape, jnp.float32),
    )
    row_peak, row_total, row_inner = lax.fori_loop(lowest, highest, first_pass, initial)
    safe_total = jnp.where(True, row_total, 1.0)
    row_delta = row_inner / safe_total
    log_total = row_peak + jnp.log(safe_total)

    def second_pass(key_block, loop_state):
        query_grad, key_accum, value_accum = loop_state
        key_rows, allowed, logits, slopes = scores_at(key_block)
        attention = jnp.where(allowed, jnp.exp(logits - log_total[..., None]), 0.0)
        score_grad = (attention * (slopes - row_delta[..., None]) * factor_scale).astype(
            jnp.bfloat16
        )
        value_part = jnp.einsum(
            "gnqk,qgnd->kgd",
            attention.astype(jnp.bfloat16),
            cotangent,
            preferred_element_type=jnp.float32,
        )
        key_part = jnp.einsum(
            "gnqk,qgnd->kgd", score_grad, queries, preferred_element_type=jnp.float32
        )
        query_grad = query_grad + jnp.einsum(
            "gnqk,kgd->qgnd", score_grad, key_rows, preferred_element_type=jnp.float32
        )
        first_row = key_block * row_count
        key_accum = lax.dynamic_update_slice_in_dim(
            key_accum,
            lax.dynamic_slice_in_dim(key_accum, first_row, row_count, 0) + key_part,
            first_row,
            0,
        )
        value_accum = lax.dynamic_update_slice_in_dim(
            value_accum,
            lax.dynamic_slice_in_dim(value_accum, first_row, row_count, 0) + value_part,
            first_row,
            0,
        )
        return (query_grad, key_accum, value_accum)

    start_grad = jnp.zeros(queries.shape, jnp.float32)
    query_grad, key_accum, value_accum = lax.fori_loop(
        lowest, highest, second_pass, (start_grad, carried[0], carried[1])
    )
    return (query_grad, (key_accum, value_accum))


def body(layer_input, query_weight, key_weight, value_weight, out_grad, doc_ids):
    tok_rows = layer_input.shape[0]
    query_width = query_weight.shape[1]
    pair_width = key_weight.shape[1]
    key_heads = pair_width // DH
    group_size = HQ // HK
    block_count = tok_rows // BLOCK
    owner_id = lax.axis_index("srv")
    weights_all = lax.all_gather(
        jnp.concatenate([query_weight, key_weight, value_weight], axis=1), "srv", axis=0, tiled=True
    )
    inputs_all = lax.all_gather(layer_input, ("hid", "rep"), axis=1, tiled=True)
    projected = jnp.dot(inputs_all, weights_all, preferred_element_type=jnp.float32).astype(
        jnp.bfloat16
    )
    queries = projected[:, :query_width].reshape(block_count, BLOCK, key_heads, group_size, DH)
    keys_local = projected[:, query_width : query_width + pair_width]
    values_local = projected[:, query_width + pair_width :]
    keys_all, values_all = (
        lax.all_gather(keys_local, "srv", axis=0, tiled=True),
        lax.all_gather(values_local, "srv", axis=0, tiled=True),
    )
    total_rows = keys_all.shape[0]
    keys_all = keys_all.reshape(total_rows, key_heads, DH)
    values_all = values_all.reshape(total_rows, key_heads, DH)
    cotangent = out_grad.reshape(block_count, BLOCK, key_heads, group_size, DH)
    empty_accum = jnp.zeros((total_rows, key_heads, DH), jnp.float32)

    def own_block(position, loop_state):
        answers, carried = loop_state
        grad_q, carried = attend(
            lax.dynamic_index_in_dim(queries, position, 0, keepdims=False),
            lax.dynamic_index_in_dim(cotangent, position, 0, keepdims=False),
            keys_all,
            values_all,
            doc_ids,
            owner_id * block_count + position,
            carried,
        )
        answers = lax.dynamic_update_index_in_dim(answers, grad_q.astype(jnp.bfloat16), position, 0)
        return (answers, carried)

    answers = jnp.zeros(queries.shape, jnp.bfloat16)
    answers, carried = lax.fori_loop(
        0, block_count, own_block, (answers, (empty_accum, empty_accum))
    )
    query_grad = answers.reshape(tok_rows, query_width)
    key_accum, value_accum = carried
    key_sum, value_sum = (
        lax.psum_scatter(key_accum, "srv", scatter_dimension=0, tiled=True),
        lax.psum_scatter(value_accum, "srv", scatter_dimension=0, tiled=True),
    )
    grads_all = jnp.concatenate(
        [
            query_grad,
            key_sum.astype(jnp.bfloat16).reshape(tok_rows, pair_width),
            value_sum.astype(jnp.bfloat16).reshape(tok_rows, pair_width),
        ],
        axis=1,
    )
    input_terms = lax.dot_general(
        grads_all, weights_all, (((1,), (1,)), ((), ())), preferred_element_type=jnp.float32
    )
    input_grad = lax.psum_scatter(
        input_terms, ("hid", "rep"), scatter_dimension=1, tiled=True
    ).astype(jnp.bfloat16)
    columns = lax.all_to_all(inputs_all, "srv", split_axis=1, concat_axis=0, tiled=True)
    weight_grad = lax.dot_general(
        columns,
        lax.all_gather(grads_all, "srv", axis=0, tiled=True),
        (((0,), (0,)), ((), ())),
        preferred_element_type=jnp.float32,
    )
    return (
        input_grad,
        weight_grad[:, :query_width],
        weight_grad[:, query_width : query_width + pair_width],
        weight_grad[:, query_width + pair_width :],
    )


MESH = pl.DeviceIdType.MESH
VM = pl.BlockSpec(memory_space=pltpu.VMEM)
VMEM_BYTES = 60 * 1024 * 1024


def place(n_rep):
    return lax.axis_index("srv"), lax.axis_index("hid") * n_rep + lax.axis_index("rep")


def device_at(z, c, n_rep):
    return {"srv": z, "hid": c // n_rep, "rep": c % n_rep}


def greet(n, m, n_rep):
    z, c = place(n_rep)
    barrier = pltpu.get_barrier_semaphore()
    for dz in range(n):
        for dc in range(m):
            if dz or dc:
                pl.semaphore_signal(
                    barrier,
                    inc=1,
                    device_id=device_at((z + dz) % n, (c + dc) % m, n_rep),
                    device_id_type=MESH,
                )
    pl.semaphore_wait(barrier, n * m - 1)


def remote(src, dst, send, recv, device):
    return pltpu.make_async_remote_copy(
        src_ref=src, dst_ref=dst, send_sem=send, recv_sem=recv, device_id=device, device_id_type=MESH
    )


def rows_at(start, size):
    return pl.ds(pl.multiple_of(start, size), size)


def cols_at(start, size):
    return pl.ds(pl.multiple_of(start, DH), size)


def attend_rows(heads, qkv, og_ref, dr_ref, dc_ref, dq_ref, dq_cols, dk, dv, first, row_block, low, width):
    q_cols = heads * DH
    scale = DH ** (-0.5)
    rows = rows_at(first, row_block)
    span = rows_at(low, row_block) if width == row_block else pl.ds(pl.multiple_of(low, row_block), width)
    queries = jnp.concatenate([qkv[rows, h * DH : (h + 1) * DH] for h in range(heads)], axis=0)
    cotangent = jnp.concatenate([og_ref[rows, h * DH : (h + 1) * DH] for h in range(heads)], axis=0)
    keys = qkv[span, q_cols : q_cols + DH]
    values = qkv[span, q_cols + DH : q_cols + 2 * DH]
    row_pos = first + lax.broadcasted_iota(jnp.int32, (row_block, width), 0)
    key_pos = low + lax.broadcasted_iota(jnp.int32, (row_block, width), 1)
    kept = (dr_ref[rows, :] == dc_ref[:, span]) & (key_pos <= row_pos)
    bias = jnp.concatenate([jnp.where(kept, 0.0, NEGATIVE)] * heads, axis=0)
    both = (((1,), (1,)), ((), ()))
    logits = lax.dot_general(queries, keys, both, preferred_element_type=jnp.float32) * scale + bias
    weights = jnp.exp(logits - jnp.max(logits, axis=1, keepdims=True))
    attention = weights * (1.0 / jnp.sum(weights, axis=1, keepdims=True))
    slopes = lax.dot_general(cotangent, values, both, preferred_element_type=jnp.float32)
    inner = jnp.sum(attention * slopes, axis=1, keepdims=True)
    score_grad = (attention * (slopes - inner) * scale).astype(jnp.bfloat16)
    down = (((0,), (0,)), ((), ()))
    query_grad = jnp.dot(score_grad, keys, preferred_element_type=jnp.float32).astype(jnp.bfloat16)
    for h in range(heads):
        dq_ref[rows, cols_at(dq_cols + h * DH, DH)] = query_grad[h * row_block : (h + 1) * row_block]
    dk[span, :] += lax.dot_general(score_grad, queries, down, preferred_element_type=jnp.float32)
    dv[span, :] += lax.dot_general(
        attention.astype(jnp.bfloat16), cotangent, down, preferred_element_type=jnp.float32
    )


def chain_kernel(
    n, m, n_rep, rows, longest,
    x_ref, og_ref, qw_ref, kw_ref, vw_ref, dr_ref, dc_ref,
    cols_ref, dqa_ref, kva_ref, ig_ref,
    rs_in, rs_out, og_own, dk, dv, terms, took, done,
    a_send, a_recv, b_send, b_recv, og_send, og_recv, rs_send, rs_recv,
    dq_send, dq_recv, kv_send, kv_recv, r_send, r_recv, e_send, e_recv,
):
    z, c = place(n_rep)
    tok, feats = x_ref.shape
    total = tok * n
    count = total // rows
    per = tok // rows
    piece = rows // m
    q_side = qw_ref.shape[1] // 2
    heads = q_side // DH
    delay = longest // rows
    lead = 2
    half = z // (n // 2)
    e = z * (1 - half) + (n - 1 - z) * half
    f = n - 1 - e
    inner = z + 1 - 2 * half
    outer = z - 1 + 2 * half
    side_b = half
    side_a = 1 - half
    near_end = (n - 1) * half
    far_end = (n - 1) * (1 - half)
    is_end = e == 0
    not_end = e > 0
    f32, bf16 = jnp.float32, jnp.bfloat16

    def chunk_rows(j):
        return rows_at(j * rows, rows)

    def input_copy(u, dq):
        q = (c + dq) % m
        src = x_ref.at[rows_at(u * rows + q * piece, piece)]
        dst = cols_ref.at[rows_at(z * tok + u * rows + q * piece, piece)]
        return src, dst, remote(
            src, dst, a_send.at[u, dq], a_recv.at[z * per + u], device_at(c, q, n_rep)
        )

    def spread_copy(j, d):
        block = cols_ref.at[rows_at(j * rows + c * piece, piece)]
        return remote(
            block, block, b_send.at[j, d], b_recv.at[j, d], device_at(z, (c + d) % m, n_rep)
        )

    def og_copy(u, s, slot, to):
        src = og_ref.at[rows_at(u * rows, rows), cols_at(s * q_side, q_side)]
        dst = og_own.at[chunk_rows(z * per + u)]
        return src, dst, remote(
            src, dst, og_send.at[u, slot], og_recv.at[z * per + u], device_at(to, c, n_rep)
        )

    def rs_copy(s, j, to):
        return remote(
            rs_out.at[s, chunk_rows(j)], rs_in.at[s, chunk_rows(j)],
            rs_send.at[s, j], rs_recv.at[s, j], device_at(to, c, n_rep),
        )

    def dq_copy(s, j, to):
        block = dqa_ref.at[chunk_rows(j), cols_at(s * q_side, q_side)]
        return remote(block, block, dq_send.at[s, j], dq_recv.at[s, j], device_at(to, c, n_rep))

    def kv_copy(s, j, to):
        block = kva_ref.at[:, chunk_rows(j), cols_at(s * DH, DH)]
        return remote(block, block, kv_send.at[s, j], kv_recv.at[s, j], device_at(to, c, n_rep))

    def term_copy(j, d):
        to = (c + d) % m
        return remote(
            terms.at[rows_at(j * rows + to * piece, piece)],
            took.at[d - 1, rows_at(j * piece, piece)],
            r_send.at[j, d], r_recv.at[j, d], device_at(z, to, n_rep),
        )

    def done_place(j):
        return ig_ref.at[rows_at((j % per) * rows + c * piece, piece)]

    def done_copy(j):
        return remote(
            done.at[rows_at(j * piece, piece)], done_place(j),
            e_send.at[j], e_recv.at[c, j % per], device_at(j // per, z, n_rep),
        )

    def spread(j):
        block = cols_ref.at[rows_at(j * rows + c * piece, piece)]
        pltpu.make_async_copy(block, block, a_recv.at[j]).wait()
        for d in range(1, m):
            spread_copy(j, d).start()

    def project(s, j):
        x = cols_ref[chunk_rows(j), :]
        return jnp.concatenate(
            [
                jnp.dot(x, qw_ref[:, cols_at(s * q_side, q_side)], preferred_element_type=f32),
                jnp.dot(x, kw_ref[:, cols_at(s * DH, DH)], preferred_element_type=f32),
                jnp.dot(x, vw_ref[:, cols_at(s * DH, DH)], preferred_element_type=f32),
            ],
            axis=1,
        )

    def reduce_a(j):
        for d in range(1, m):
            spread_copy(j, d).wait_recv()
        part = project(side_a, j)

        @pl.when(is_end)
        def _():
            rs_out[side_a, chunk_rows(j), :] = part.astype(bf16)

        @pl.when(not_end)
        def _():
            rs_copy(side_a, j, inner).wait_recv()
            rs_out[side_a, chunk_rows(j), :] = (
                part + rs_in[side_a, chunk_rows(j), :].astype(f32)
            ).astype(bf16)

        rs_copy(side_a, j, inner).start()

    def reduce_b(j):
        part = project(side_b, j)
        rs_copy(side_b, j, inner).wait_recv()
        rs_out[side_b, chunk_rows(j), :] = (
            part + rs_in[side_b, chunk_rows(j), :].astype(f32)
        ).astype(bf16)

        @pl.when(not_end)
        def _():
            rs_copy(side_b, j, outer).start()

    def settle(i):
        kva_ref[0, chunk_rows(i), cols_at(side_b * DH, DH)] = dk[chunk_rows(i), :].astype(bf16)
        kva_ref[1, chunk_rows(i), cols_at(side_b * DH, DH)] = dv[chunk_rows(i), :].astype(bf16)
        kv_copy(side_b, i, inner).start()

    def attend_chunk(j):
        block = og_own.at[chunk_rows(j)]
        pltpu.make_async_copy(block, block, og_recv.at[j]).wait()
        run = functools.partial(
            attend_rows, heads, rs_out.at[side_b], og_own, dr_ref, dc_ref, dqa_ref, side_b * q_side, dk, dv
        )
        for b in range(delay):
            @pl.when(j == b)
            def _():
                run(b * rows, rows, 0, (b + 1) * rows)

        @pl.when(j >= delay)
        def _():
            run(j * rows, rows, (j - delay) * rows, (delay + 1) * rows)

        dq_copy(side_b, j, inner).start()

        @pl.when(j >= delay)
        def _():
            settle(j - delay)

        @pl.when(j == count - 1)
        def _():
            def rest(i, carry):
                settle(i)
                return carry

            lax.fori_loop(count - delay, count, rest, 0)

    def finish(j):
        for d in range(1, m):
            term_copy(j, d).wait_recv()
        value = terms[rows_at(j * rows + c * piece, piece), :].astype(f32)
        for d in range(1, m):
            value = value + took[d - 1, rows_at(j * piece, piece), :].astype(f32)
        done[rows_at(j * piece, piece), :] = value.astype(bf16)
        own = (j // per == z) & (c == z)

        @pl.when(own)
        def _():
            pltpu.make_async_copy(
                done.at[rows_at(j * piece, piece)], done_place(j), e_recv.at[c, j % per]
            ).start()

        @pl.when(jnp.logical_not(own))
        def _():
            done_copy(j).start()

    def term(j):
        across = (((1,), (1,)), ((), ()))
        value = lax.dot_general(
            dqa_ref[chunk_rows(j), :], qw_ref[...], across, preferred_element_type=f32
        )
        value = value + lax.dot_general(
            kva_ref[0, chunk_rows(j), :], kw_ref[...], across, preferred_element_type=f32
        )
        value = value + lax.dot_general(
            kva_ref[1, chunk_rows(j), :], vw_ref[...], across, preferred_element_type=f32
        )
        terms[chunk_rows(j), :] = value.astype(bf16)
        for d in range(1, m):
            term_copy(j, d).start()

        @pl.when(j > 0)
        def _():
            finish(j - 1)

    def pass_pair_b(i):
        kv_copy(side_b, i, inner).wait_recv()
        kv_copy(side_b, i, inner).start()

    def pass_pair_a(i):
        kv_copy(side_a, i, inner).wait_recv()

        @pl.when(not_end)
        def _():
            kv_copy(side_a, i, outer).start()

        term(i)

    greet(n, m, n_rep)
    own = c == z
    for u in range(per):
        for dq in range(m):
            src, dst, copy = input_copy(u, dq)
            if dq == 0:
                @pl.when(own)
                def _():
                    pltpu.make_async_copy(src, dst, a_recv.at[z * per + u]).start()

                @pl.when(jnp.logical_not(own))
                def _():
                    copy.start()
            else:
                copy.start()

    @pl.when(is_end)
    def _():
        dk[...] = jnp.zeros_like(dk)
        dv[...] = jnp.zeros_like(dv)

    for j in range(lead):
        spread(j)

    def step(k, carry):
        u = k - z * per

        @pl.when((k >= z * per) & (k < z * per + per))
        def _():
            _, _, copy = og_copy(u, side_a, 0, far_end)
            copy.start()
            src, dst, copy = og_copy(u, side_b, 1, near_end)

            @pl.when(is_end)
            def _():
                pltpu.make_async_copy(src, dst, og_recv.at[z * per + u]).start()

            @pl.when(not_end)
            def _():
                copy.start()

        @pl.when((k >= e) & (k < e + count))
        def _():
            reduce_a(k - e)

        @pl.when(k + lead < count)
        def _():
            spread(k + lead)

        @pl.when((k >= f) & (k < f + count))
        def _():
            reduce_b(k - f)

        @pl.when(is_end & (k >= n - 1) & (k < n - 1 + count))
        def _():
            attend_chunk(k - (n - 1))

        jb = k - (n - 1) - e

        @pl.when(not_end & (k >= n - 1 + e) & (k < n - 1 + e + count))
        def _():
            dq_copy(side_b, jb, inner).wait_recv()
            dq_copy(side_b, jb, inner).start()

            @pl.when(jb >= delay)
            def _():
                pass_pair_b(jb - delay)

            @pl.when(jb == count - 1)
            def _():
                def rest(i, carry):
                    pass_pair_b(i)
                    return carry

                lax.fori_loop(count - delay, count, rest, 0)

        ja = k - (n - 1) - f

        @pl.when((k >= n - 1 + f) & (k < n - 1 + f + count))
        def _():
            dq_copy(side_a, ja, inner).wait_recv()

            @pl.when(not_end)
            def _():
                dq_copy(side_a, ja, outer).start()

            @pl.when(ja >= delay)
            def _():
                first = ja - delay
                last = first + 1 + delay * (ja // (count - 1))

                def rest(i, carry):
                    pass_pair_a(i)
                    return carry

                lax.fori_loop(first, last, rest, 0)

        return carry

    lax.fori_loop(0, count + 2 * (n - 1), step, 0)
    finish(jnp.int32(count - 1))

    def drain(j, carry):
        for d in range(1, m):
            spread_copy(j, d).wait_send()
            term_copy(j, d).wait_send()
        rs_copy(side_a, j, inner).wait_send()
        dq_copy(side_b, j, inner).wait_send()
        kv_copy(side_b, j, inner).wait_send()

        @pl.when(not_end)
        def _():
            rs_copy(side_b, j, outer).wait_send()
            dq_copy(side_a, j, outer).wait_send()
            kv_copy(side_a, j, outer).wait_send()

        @pl.when(jnp.logical_not((j // per == z) & (c == z)))
        def _():
            done_copy(j).wait_send()

        return carry

    lax.fori_loop(0, count, drain, 0)
    for u in range(per):
        _, _, copy = og_copy(u, side_a, 0, far_end)
        copy.wait_send()

        @pl.when(not_end)
        def _():
            _, _, copy = og_copy(u, side_b, 1, near_end)
            copy.wait_send()

        for dq in range(m):
            _, _, copy = input_copy(u, dq)
            if dq == 0:
                @pl.when(jnp.logical_not(own))
                def _():
                    copy.wait_send()
            else:
                copy.wait_send()
        for q in range(m):
            block = ig_ref.at[u * rows + q * piece : u * rows + (q + 1) * piece]
            pltpu.make_async_copy(block, block, e_recv.at[q, u]).wait()


def chained(n, n_hid, n_rep, layer_input, query_weight, key_weight, value_weight, out_grad, doc_ids):
    m = n_hid * n_rep
    bf16, f32 = jnp.bfloat16, jnp.float32
    tok, feats = layer_input.shape
    total = tok * n
    rows = BLOCK
    count, per, piece = total // rows, tok // rows, rows // m
    q_cols = query_weight.shape[1]
    pair_width = key_weight.shape[1]
    width = q_cols // 2 + pair_width
    dma = pltpu.SemaphoreType.DMA
    columns, queries_all, pairs_all, input_grad = pl.pallas_call(
        functools.partial(chain_kernel, n, m, n_rep, rows, total // 2),
        out_shape=(
            jax.ShapeDtypeStruct((total, feats), bf16),
            jax.ShapeDtypeStruct((total, q_cols), bf16),
            jax.ShapeDtypeStruct((2, total, pair_width), bf16),
            jax.ShapeDtypeStruct((tok, feats), bf16),
        ),
        in_specs=[VM] * 7,
        out_specs=(VM,) * 4,
        scratch_shapes=[
            pltpu.VMEM((2, total, width), bf16),
            pltpu.VMEM((2, total, width), bf16),
            pltpu.VMEM((total, q_cols // 2), bf16),
            pltpu.VMEM((total, DH), f32),
            pltpu.VMEM((total, DH), f32),
            pltpu.VMEM((total, feats), bf16),
            pltpu.VMEM((m - 1, count * piece, feats), bf16),
            pltpu.VMEM((count * piece, feats), bf16),
            dma((per, m)), dma((count,)), dma((count, m)), dma((count, m)),
            dma((per, 2)), dma((count,)), dma((2, count)), dma((2, count)),
            dma((2, count)), dma((2, count)), dma((2, count)), dma((2, count)),
            dma((count, m)), dma((count, m)), dma((count,)), dma((m, per)),
        ],
        compiler_params=pltpu.CompilerParams(
            collective_id=0, has_side_effects=True, vmem_limit_bytes=VMEM_BYTES
        ),
    )(
        layer_input, out_grad, query_weight, key_weight, value_weight,
        doc_ids.reshape(total, 1), doc_ids.reshape(1, total),
    )

    def weight_grad(grads):
        return lax.dot_general(
            columns, grads, (((0,), (0,)), ((), ())), preferred_element_type=f32
        )

    return (
        input_grad,
        weight_grad(queries_all),
        weight_grad(pairs_all[0]),
        weight_grad(pairs_all[1]),
    )


def solution(mesh):
    in_specs = (
        P(("groups", "srv"), ("hid", "rep")),
        P("srv", ("hid", "rep")),
        P("srv", ("hid", "rep")),
        P("srv", ("hid", "rep")),
        P(("groups", "srv"), ("hid", "rep")),
        P("groups"),
    )
    out_specs = (
        P(("groups", "srv"), ("hid", "rep")),
        P(("groups", "srv"), ("hid", "rep")),
        P(("groups", "srv"), ("hid", "rep")),
        P(("groups", "srv"), ("hid", "rep")),
    )
    n, n_hid, n_rep = mesh.shape["srv"], mesh.shape["hid"], mesh.shape["rep"]
    m = n_hid * n_rep
    inner = body
    if n == m and n > 2 and n % 2 == 0 and HK == 2 * m and HQ % HK == 0:
        inner = functools.partial(chained, n, n_hid, n_rep)
    return jax.shard_map(inner, mesh=mesh, in_specs=in_specs, out_specs=out_specs, check_vma=False)
```

```python
import functools

import jax
import jax.numpy as jnp
from jax import lax
from jax.experimental import pallas as pl
from jax.experimental.pallas import tpu as pltpu
from jax.sharding import PartitionSpec as P

HQ = 32
HK = 8
DH = 128
BLOCK = 128


NEGATIVE = -1e30


def attend(queries, cotangent, keys_all, values_all, doc_ids, block_id, carried):
    row_count = queries.shape[0]
    factor_scale = queries.shape[-1] ** (-0.5)
    offsets = jnp.arange(row_count, dtype=jnp.int32)
    query_pos = block_id * row_count + offsets
    query_doc = lax.dynamic_slice_in_dim(doc_ids, block_id * row_count, row_count)
    doc_start = jnp.sum((doc_ids < query_doc[0]).astype(jnp.int32))
    lowest = doc_start // row_count
    highest = jnp.where(True, block_id + 1, lowest)

    def scores_at(key_block):
        key_rows = lax.dynamic_slice_in_dim(keys_all, key_block * row_count, row_count, 0)
        value_rows = lax.dynamic_slice_in_dim(values_all, key_block * row_count, row_count, 0)
        key_doc = lax.dynamic_slice_in_dim(doc_ids, key_block * row_count, row_count)
        key_pos = key_block * row_count + offsets
        allowed = (key_doc[None, :] == query_doc[:, None]) & (
            key_pos[None, :] <= query_pos[:, None]
        )
        logits = (
            jnp.einsum("qgnd,kgd->gnqk", queries, key_rows, preferred_element_type=jnp.float32)
            * factor_scale
        )
        logits = jnp.where(allowed, logits, NEGATIVE)
        slopes = jnp.einsum(
            "qgnd,kgd->gnqk", cotangent, value_rows, preferred_element_type=jnp.float32
        )
        return (key_rows, allowed, logits, slopes)

    def first_pass(key_block, loop_state):
        row_peak, row_total, row_inner = loop_state
        key_rows, allowed, logits, slopes = scores_at(key_block)
        new_peak = jnp.maximum(row_peak, jnp.max(logits, axis=-1))
        weights = jnp.where(allowed, jnp.exp(logits - new_peak[..., None]), 0.0)
        factor = jnp.exp(row_peak - new_peak)
        row_total = row_total * factor + jnp.sum(weights, axis=-1)
        row_inner = row_inner * factor + jnp.sum(weights * slopes, axis=-1)
        return (new_peak, row_total, row_inner)

    stat_shape = (queries.shape[1], queries.shape[2], row_count)
    initial = (
        jnp.full(stat_shape, NEGATIVE, jnp.float32),
        jnp.zeros(stat_shape, jnp.float32),
        jnp.zeros(stat_shape, jnp.float32),
    )
    row_peak, row_total, row_inner = lax.fori_loop(lowest, highest, first_pass, initial)
    safe_total = jnp.where(True, row_total, 1.0)
    row_delta = row_inner / safe_total
    log_total = row_peak + jnp.log(safe_total)

    def second_pass(key_block, loop_state):
        query_grad, key_accum, value_accum = loop_state
        key_rows, allowed, logits, slopes = scores_at(key_block)
        attention = jnp.where(allowed, jnp.exp(logits - log_total[..., None]), 0.0)
        score_grad = (attention * (slopes - row_delta[..., None]) * factor_scale).astype(
            jnp.bfloat16
        )
        value_part = jnp.einsum(
            "gnqk,qgnd->kgd",
            attention.astype(jnp.bfloat16),
            cotangent,
            preferred_element_type=jnp.float32,
        )
        key_part = jnp.einsum(
            "gnqk,qgnd->kgd", score_grad, queries, preferred_element_type=jnp.float32
        )
        query_grad = query_grad + jnp.einsum(
            "gnqk,kgd->qgnd", score_grad, key_rows, preferred_element_type=jnp.float32
        )
        first_row = key_block * row_count
        key_accum = lax.dynamic_update_slice_in_dim(
            key_accum,
            lax.dynamic_slice_in_dim(key_accum, first_row, row_count, 0) + key_part,
            first_row,
            0,
        )
        value_accum = lax.dynamic_update_slice_in_dim(
            value_accum,
            lax.dynamic_slice_in_dim(value_accum, first_row, row_count, 0) + value_part,
            first_row,
            0,
        )
        return (query_grad, key_accum, value_accum)

    start_grad = jnp.zeros(queries.shape, jnp.float32)
    query_grad, key_accum, value_accum = lax.fori_loop(
        lowest, highest, second_pass, (start_grad, carried[0], carried[1])
    )
    return (query_grad, (key_accum, value_accum))


def body(layer_input, query_weight, key_weight, value_weight, out_grad, doc_ids):
    tok_rows = layer_input.shape[0]
    query_width = query_weight.shape[1]
    pair_width = key_weight.shape[1]
    key_heads = pair_width // DH
    group_size = HQ // HK
    block_count = tok_rows // BLOCK
    owner_id = lax.axis_index("srv")
    weights_all = lax.all_gather(
        jnp.concatenate([query_weight, key_weight, value_weight], axis=1), "srv", axis=0, tiled=True
    )
    inputs_all = lax.all_gather(layer_input, ("hid", "rep"), axis=1, tiled=True)
    projected = jnp.dot(inputs_all, weights_all, preferred_element_type=jnp.float32).astype(
        jnp.bfloat16
    )
    queries = projected[:, :query_width].reshape(block_count, BLOCK, key_heads, group_size, DH)
    keys_local = projected[:, query_width : query_width + pair_width]
    values_local = projected[:, query_width + pair_width :]
    keys_all, values_all = (
        lax.all_gather(keys_local, "srv", axis=0, tiled=True),
        lax.all_gather(values_local, "srv", axis=0, tiled=True),
    )
    total_rows = keys_all.shape[0]
    keys_all = keys_all.reshape(total_rows, key_heads, DH)
    values_all = values_all.reshape(total_rows, key_heads, DH)
    cotangent = out_grad.reshape(block_count, BLOCK, key_heads, group_size, DH)
    empty_accum = jnp.zeros((total_rows, key_heads, DH), jnp.float32)

    def own_block(position, loop_state):
        answers, carried = loop_state
        grad_q, carried = attend(
            lax.dynamic_index_in_dim(queries, position, 0, keepdims=False),
            lax.dynamic_index_in_dim(cotangent, position, 0, keepdims=False),
            keys_all,
            values_all,
            doc_ids,
            owner_id * block_count + position,
            carried,
        )
        answers = lax.dynamic_update_index_in_dim(answers, grad_q.astype(jnp.bfloat16), position, 0)
        return (answers, carried)

    answers = jnp.zeros(queries.shape, jnp.bfloat16)
    answers, carried = lax.fori_loop(
        0, block_count, own_block, (answers, (empty_accum, empty_accum))
    )
    query_grad = answers.reshape(tok_rows, query_width)
    key_accum, value_accum = carried
    key_sum, value_sum = (
        lax.psum_scatter(key_accum, "srv", scatter_dimension=0, tiled=True),
        lax.psum_scatter(value_accum, "srv", scatter_dimension=0, tiled=True),
    )
    grads_all = jnp.concatenate(
        [
            query_grad,
            key_sum.astype(jnp.bfloat16).reshape(tok_rows, pair_width),
            value_sum.astype(jnp.bfloat16).reshape(tok_rows, pair_width),
        ],
        axis=1,
    )
    input_terms = lax.dot_general(
        grads_all, weights_all, (((1,), (1,)), ((), ())), preferred_element_type=jnp.float32
    )
    input_grad = lax.psum_scatter(
        input_terms, ("hid", "rep"), scatter_dimension=1, tiled=True
    ).astype(jnp.bfloat16)
    columns = lax.all_to_all(inputs_all, "srv", split_axis=1, concat_axis=0, tiled=True)
    weight_grad = lax.dot_general(
        columns,
        lax.all_gather(grads_all, "srv", axis=0, tiled=True),
        (((0,), (0,)), ((), ())),
        preferred_element_type=jnp.float32,
    )
    return (
        input_grad,
        weight_grad[:, :query_width],
        weight_grad[:, query_width : query_width + pair_width],
        weight_grad[:, query_width + pair_width :],
    )


MESH = pl.DeviceIdType.MESH
VM = pl.BlockSpec(memory_space=pltpu.VMEM)
VMEM_BYTES = 60 * 1024 * 1024


def place(n_rep):
    return lax.axis_index("srv"), lax.axis_index("hid") * n_rep + lax.axis_index("rep")


def device_at(z, c, n_rep):
    return {"srv": z, "hid": c // n_rep, "rep": c % n_rep}


def greet(n, m, n_rep):
    z, c = place(n_rep)
    barrier = pltpu.get_barrier_semaphore()
    for dz in range(n):
        for dc in range(m):
            if dz or dc:
                pl.semaphore_signal(
                    barrier,
                    inc=1,
                    device_id=device_at((z + dz) % n, (c + dc) % m, n_rep),
                    device_id_type=MESH,
                )
    pl.semaphore_wait(barrier, n * m - 1)


def remote(src, dst, send, recv, device):
    return pltpu.make_async_remote_copy(
        src_ref=src, dst_ref=dst, send_sem=send, recv_sem=recv, device_id=device, device_id_type=MESH
    )


def rows_at(start, size):
    return pl.ds(pl.multiple_of(start, size), size)


def cols_at(start, size):
    return pl.ds(pl.multiple_of(start, DH), size)


def attend_rows(heads, qkv, og_ref, dc_ref, dq_ref, dq_cols, dk, dv, first, row_block, low, width):
    q_cols = heads * DH
    scale = DH ** (-0.5)
    rows = rows_at(first, row_block)
    span = rows_at(low, row_block) if width == row_block else pl.ds(pl.multiple_of(low, row_block), width)
    queries = jnp.concatenate([qkv[rows, h * DH : (h + 1) * DH] for h in range(heads)], axis=0)
    cotangent = jnp.concatenate([og_ref[rows, h * DH : (h + 1) * DH] for h in range(heads)], axis=0)
    keys = qkv[span, q_cols : q_cols + DH]
    values = qkv[span, q_cols + DH : q_cols + 2 * DH]
    row_pos = first + lax.broadcasted_iota(jnp.int32, (row_block, width), 0)
    key_pos = low + lax.broadcasted_iota(jnp.int32, (row_block, width), 1)
    row_doc = jnp.broadcast_to(dc_ref[:, rows].astype(jnp.float32), (row_block, row_block)).T[:, :1]
    kept = (row_doc == dc_ref[:, span].astype(jnp.float32)) & (key_pos <= row_pos)
    bias = jnp.concatenate([jnp.where(kept, 0.0, NEGATIVE)] * heads, axis=0)
    both = (((1,), (1,)), ((), ()))
    logits = lax.dot_general(queries, keys, both, preferred_element_type=jnp.float32) * scale + bias
    weights = jnp.exp(logits - jnp.max(logits, axis=1, keepdims=True))
    attention = weights * (1.0 / jnp.sum(weights, axis=1, keepdims=True))
    slopes = lax.dot_general(cotangent, values, both, preferred_element_type=jnp.float32)
    inner = jnp.sum(attention * slopes, axis=1, keepdims=True)
    score_grad = (attention * (slopes - inner) * scale).astype(jnp.bfloat16)
    down = (((0,), (0,)), ((), ()))
    query_grad = jnp.dot(score_grad, keys, preferred_element_type=jnp.float32).astype(jnp.bfloat16)
    for h in range(heads):
        dq_ref[rows, cols_at(dq_cols + h * DH, DH)] = query_grad[h * row_block : (h + 1) * row_block]
    dk[span, :] += lax.dot_general(score_grad, queries, down, preferred_element_type=jnp.float32)
    dv[span, :] += lax.dot_general(
        attention.astype(jnp.bfloat16), cotangent, down, preferred_element_type=jnp.float32
    )


def chain_kernel(
    n, m, n_rep, rows, longest,
    x_ref, og_ref, qw_in, kw_in, vw_in, dc_ref,
    turned_out, dqa_out, kva_out, ig_ref,
    qw_ref, kw_ref, vw_ref, cols_ref, turned, dqa_ref, kva_ref, rs_in, rs_out, og_own, dk, dv, hopped, terms, took, paired, done,
    h_send, h_recv, a_send, a_recv, b_send, b_recv, og_send, og_recv, rs_send, rs_recv,
    dq_send, dq_recv, kv_send, kv_recv, r_send, r_recv, e_send, e_recv, out_sem, w_sem,
):
    z, c = place(n_rep)
    tok, feats = x_ref.shape
    total = tok * n
    count = total // rows
    per = tok // rows
    piece = rows // m
    parts = tok // (rows // 2)
    share = piece // 2
    q_side = qw_ref.shape[1] // 2
    heads = q_side // DH
    delay = longest // rows
    lead = 5
    half = z // (n // 2)
    e = z * (1 - half) + (n - 1 - z) * half
    f = n - 1 - e
    inner = z + 1 - 2 * half
    outer = z - 1 + 2 * half
    side_b = half
    side_a = 1 - half
    near_end = (n - 1) * half
    far_end = (n - 1) * (1 - half)
    is_end = e == 0
    not_end = e > 0
    sibling = c + 1 - 2 * (c % 2)
    across = (c + 2) % m
    diagonal = across + 1 - 2 * (across % 2)
    sub = rows // 2
    f32, bf16 = jnp.float32, jnp.bfloat16

    def chunk_rows(j):
        return rows_at(j * rows, rows)

    def hop_copy(u):
        src = x_ref.at[rows_at(u * sub + (across // 2) * 2 * share, 2 * share)]
        return remote(src, hopped.at[u], h_send.at[u], h_recv.at[u], device_at(z, across, n_rep))

    def input_copy(u, i, direct):
        p = (c // 2) * 2 + i
        plane = c if direct else across
        if direct:
            src = x_ref.at[rows_at(u * sub + p * share, share)]
        else:
            src = hopped.at[u, i * share : (i + 1) * share]
        dst = cols_ref.at[rows_at(z * tok + u * sub + p * share, share)]
        copy = remote(
            src, dst, a_send.at[u, i, int(direct)], a_recv.at[z * parts + u], device_at(plane, p, n_rep)
        )
        return (plane == z) & (p == c), src, dst, copy

    def send_input(u, i, direct):
        own, src, dst, copy = input_copy(u, i, direct)

        @pl.when(own)
        def _():
            pltpu.make_async_copy(src, dst, a_recv.at[z * parts + u]).start()

        @pl.when(jnp.logical_not(own))
        def _():
            copy.start()

    def spread_copy(g, slot):
        owner, to = ((c, sibling), (c, across), (across, sibling))[slot]
        block = cols_ref.at[rows_at(g * sub + owner * share, share)]
        return remote(
            block, block, b_send.at[g, slot], b_recv.at[g, slot], device_at(z, to, n_rep)
        )

    def og_copy(u, s, slot, to):
        src = og_ref.at[rows_at(u * rows, rows), cols_at(s * q_side, q_side)]
        dst = og_own.at[chunk_rows(z * per + u)]
        return src, dst, remote(
            src, dst, og_send.at[u, slot], og_recv.at[z * per + u], device_at(to, c, n_rep)
        )

    def sub_rows(g):
        return rows_at(g * sub, sub)

    def rs_copy(s, g, to):
        return remote(
            rs_out.at[s, sub_rows(g)], rs_in.at[s, sub_rows(g)],
            rs_send.at[s, g], rs_recv.at[s, g], device_at(to, c, n_rep),
        )

    def dq_copy(s, j, to):
        block = dqa_ref.at[chunk_rows(j), cols_at(s * q_side, q_side)]
        return remote(block, block, dq_send.at[s, j], dq_recv.at[s, j], device_at(to, c, n_rep))

    def kv_copy(s, j, to):
        block = kva_ref.at[:, chunk_rows(j), cols_at(s * DH, DH)]
        return remote(block, block, kv_send.at[s, j], kv_recv.at[s, j], device_at(to, c, n_rep))

    def term_rows(j, owner):
        return rows_at(j * rows + owner * piece, piece)

    def term_copy(j, slot):
        return remote(
            terms.at[term_rows(j, diagonal if slot else sibling)],
            took.at[slot, rows_at(j * piece, piece)],
            r_send.at[j, slot], r_recv.at[j, slot], device_at(z, sibling, n_rep),
        )

    def pair_copy(j):
        block = rows_at(j * piece, piece)
        return remote(
            paired.at[block], took.at[2, block],
            r_send.at[j, 2], r_recv.at[j, 2], device_at(z, across, n_rep),
        )

    def done_place(j):
        return ig_ref.at[rows_at((j % per) * rows + c * piece, piece)]

    def done_copy(j):
        return remote(
            done.at[rows_at(j * piece, piece)], done_place(j),
            e_send.at[j], e_recv.at[c, j % per], device_at(j // per, z, n_rep),
        )

    def spread(g):
        block = cols_ref.at[rows_at(g * sub + c * share, share)]
        pltpu.make_async_copy(block, block, a_recv.at[g]).wait()
        for slot in (1, 0):
            spread_copy(g, slot).start()

    def relay(j):
        spread_copy(j, 1).wait_recv()
        spread_copy(j, 2).start()

    def project(s, g):
        x = cols_ref[sub_rows(g), :]
        return jnp.concatenate(
            [
                jnp.dot(x, qw_ref[:, cols_at(s * q_side, q_side)], preferred_element_type=f32),
                jnp.dot(x, kw_ref[:, cols_at(s * DH, DH)], preferred_element_type=f32),
                jnp.dot(x, vw_ref[:, cols_at(s * DH, DH)], preferred_element_type=f32),
            ],
            axis=1,
        )

    def add_in(s, g):
        part = project(s, g)
        rs_copy(s, g, inner).wait_recv()
        rs_out[s, sub_rows(g), :] = (part + rs_in[s, sub_rows(g), :].astype(f32)).astype(bf16)

    def out_copy(j, slot):
        if slot == 2:
            src, dst = kva_ref.at[:, chunk_rows(j)], kva_out.at[:, chunk_rows(j)]
        elif slot == 1:
            src, dst = dqa_ref.at[chunk_rows(j)], dqa_out.at[chunk_rows(j)]
        else:
            src, dst = turned.at[:, chunk_rows(j)], turned_out.at[:, chunk_rows(j)]
        return pltpu.make_async_copy(src, dst, out_sem.at[j, slot])

    def reduce_a(g):
        for slot in (0, 2):
            spread_copy(g, slot).wait_recv()

        @pl.when(is_end)
        def _():
            rs_out[side_a, sub_rows(g), :] = project(side_a, g).astype(bf16)

        @pl.when(not_end)
        def _():
            add_in(side_a, g)

        rs_copy(side_a, g, inner).start()

    def reduce_b(g):
        add_in(side_b, g)

        @pl.when(not_end)
        def _():
            rs_copy(side_b, g, outer).start()

    def settle(i):
        kva_ref[0, chunk_rows(i), cols_at(side_b * DH, DH)] = dk[chunk_rows(i), :].astype(bf16)
        kva_ref[1, chunk_rows(i), cols_at(side_b * DH, DH)] = dv[chunk_rows(i), :].astype(bf16)
        kv_copy(side_b, i, inner).start()

    def attend_chunk(j):
        block = og_own.at[chunk_rows(j)]
        pltpu.make_async_copy(block, block, og_recv.at[j]).wait()
        run = functools.partial(
            attend_rows, heads, rs_out.at[side_b], og_own, dc_ref, dqa_ref, side_b * q_side, dk, dv
        )
        for b in range(delay):
            @pl.when(j == b)
            def _():
                run(b * rows, rows, 0, (b + 1) * rows)

        @pl.when(j >= delay)
        def _():
            run(j * rows, rows, (j - delay) * rows, (delay + 1) * rows)

        dq_copy(side_b, j, inner).start()

        @pl.when(j >= delay)
        def _():
            settle(j - delay)

        @pl.when(j == count - 1)
        def _():
            def rest(i, carry):
                settle(i)
                return carry

            lax.fori_loop(count - delay, count, rest, 0)

    def combine(j):
        term_copy(j, 1).wait_recv()
        block = rows_at(j * piece, piece)
        value = terms[term_rows(j, across), :].astype(f32) + took[1, block, :].astype(f32)
        paired[block, :] = value.astype(bf16)
        pair_copy(j).start()

    def finish(j):
        block = rows_at(j * piece, piece)
        term_copy(j, 0).wait_recv()
        value = terms[term_rows(j, c), :].astype(f32) + took[0, block, :].astype(f32)
        pair_copy(j).wait_recv()
        value = value + took[2, block, :].astype(f32)
        done[rows_at(j * piece, piece), :] = value.astype(bf16)
        own = (j // per == z) & (c == z)

        @pl.when(own)
        def _():
            pltpu.make_async_copy(
                done.at[rows_at(j * piece, piece)], done_place(j), e_recv.at[c, j % per]
            ).start()

        @pl.when(jnp.logical_not(own))
        def _():
            done_copy(j).start()

    def term(j):
        for slot in (1, 2):
            out_copy(j, slot).start()
        flip = (((1,), (1,)), ((), ()))
        value = lax.dot_general(
            dqa_ref[chunk_rows(j), :], qw_ref[...], flip, preferred_element_type=f32
        )
        value = value + lax.dot_general(
            kva_ref[0, chunk_rows(j), :], kw_ref[...], flip, preferred_element_type=f32
        )
        value = value + lax.dot_general(
            kva_ref[1, chunk_rows(j), :], vw_ref[...], flip, preferred_element_type=f32
        )
        terms[chunk_rows(j), :] = value.astype(bf16)
        for slot in (1, 0):
            term_copy(j, slot).start()

        @pl.when(j > 0)
        def _():
            combine(j - 1)

        @pl.when(j > 1)
        def _():
            finish(j - 2)

    def pass_b(v):
        @pl.when(v < count)
        def _():
            dq_copy(side_b, v, inner).wait_recv()
            dq_copy(side_b, v, inner).start()

        @pl.when(v >= delay)
        def _():
            kv_copy(side_b, v - delay, inner).wait_recv()
            kv_copy(side_b, v - delay, inner).start()

    def pass_a(v):
        @pl.when(v < count)
        def _():
            dq_copy(side_a, v, inner).wait_recv()

            @pl.when(not_end)
            def _():
                dq_copy(side_a, v, outer).start()

        @pl.when(v >= delay)
        def _():
            kv_copy(side_a, v - delay, inner).wait_recv()

            @pl.when(not_end)
            def _():
                kv_copy(side_a, v - delay, outer).start()

            term(v - delay)

    loads = [
        pltpu.make_async_copy(qw_in, qw_ref, w_sem.at[0]),
        pltpu.make_async_copy(kw_in, kw_ref, w_sem.at[1]),
        pltpu.make_async_copy(vw_in, vw_ref, w_sem.at[2]),
    ]
    for copy in loads:
        copy.start()
    greet(n, m, n_rep)
    for u in range(parts):
        hop_copy(u).start()
    for u in range(parts):
        for i in range(2):
            send_input(u, i, True)

    @pl.when(is_end)
    def _():
        dk[...] = jnp.zeros_like(dk)
        dv[...] = jnp.zeros_like(dv)

    def forward(u):
        hop_copy(u).wait_recv()
        for i in range(2):
            send_input(u, i, False)

    def send_og(u, slot):
        to = (far_end, near_end)[slot]
        src, dst, copy = og_copy(u, (side_a, side_b)[slot], slot, to)
        if slot == 0:
            copy.start()
        else:
            @pl.when(is_end)
            def _():
                pltpu.make_async_copy(src, dst, og_recv.at[z * per + u]).start()

            @pl.when(not_end)
            def _():
                copy.start()

    forward(0)
    forward(1)
    spread(0)
    for u in range(2, parts):
        forward(u)
    for g in range(1, lead):
        spread(g)
    for g in range(2):
        relay(g)
    for u in range(per):
        send_og(u, 1)

        @pl.when(not_end)
        def _():
            send_og(u, 0)
    for copy in loads:
        copy.wait()

    def step(k, carry):
        even = k % 2 == 0
        j = k // 2

        @pl.when(is_end & even & (j > 0) & (j <= per))
        def _():
            send_og(j - 1, 0)

        @pl.when(k + 2 < 2 * count)
        def _():
            relay(k + 2)

        @pl.when((k >= 2 * e) & (k < 2 * e + 2 * count))
        def _():
            reduce_a(k - 2 * e)

        @pl.when(k + lead < 2 * count)
        def _():
            spread(k + lead)

        @pl.when((k % 2 == 1) & (k >= 2 * e) & (k < 2 * e + 2 * count))
        def _():
            turned[:, chunk_rows(j - e)] = cols_ref[chunk_rows(j - e), :].T
            out_copy(j - e, 0).start()

        @pl.when((k >= 2 * f) & (k < 2 * f + 2 * count))
        def _():
            reduce_b(k - 2 * f)

        h = j + 1

        @pl.when(is_end & (k % 2 == 1) & (h >= n) & (h < n + count))
        def _():
            attend_chunk(h - n)

        @pl.when(not_end & (k % 2 == 1) & (h >= n + e) & (h < n + e + count + delay))
        def _():
            pass_b(h - n - e)

        @pl.when((k % 2 == 1) & (h >= n + f) & (h < n + f + count + delay))
        def _():
            pass_a(h - n - f)

        return carry

    lax.fori_loop(0, 2 * (count + delay + 2 * (n - 1) + 1), step, 0)
    combine(jnp.int32(count - 1))
    finish(jnp.int32(count - 2))
    finish(jnp.int32(count - 1))

    def drain(j, carry):
        for slot in range(3):
            spread_copy(2 * j, slot).wait_send()
            spread_copy(2 * j + 1, slot).wait_send()
        for slot in range(2):
            term_copy(j, slot).wait_send()
        pair_copy(j).wait_send()
        for i in range(2):
            rs_copy(side_a, 2 * j + i, inner).wait_send()
        for slot in range(3):
            out_copy(j, slot).wait()
        dq_copy(side_b, j, inner).wait_send()
        kv_copy(side_b, j, inner).wait_send()

        @pl.when(not_end)
        def _():
            for i in range(2):
                rs_copy(side_b, 2 * j + i, outer).wait_send()
            dq_copy(side_a, j, outer).wait_send()
            kv_copy(side_a, j, outer).wait_send()

        @pl.when(jnp.logical_not((j // per == z) & (c == z)))
        def _():
            done_copy(j).wait_send()

        return carry

    lax.fori_loop(0, count, drain, 0)
    for u in range(parts):
        hop_copy(u).wait_send()
        for i in range(2):
            for direct in (True, False):
                own, _, _, copy = input_copy(u, i, direct)

                @pl.when(jnp.logical_not(own))
                def _():
                    copy.wait_send()
    for u in range(per):
        _, _, copy = og_copy(u, side_a, 0, far_end)
        copy.wait_send()

        @pl.when(not_end)
        def _():
            _, _, copy = og_copy(u, side_b, 1, near_end)
            copy.wait_send()

        for q in range(m):
            block = ig_ref.at[u * rows + q * piece : u * rows + (q + 1) * piece]
            pltpu.make_async_copy(block, block, e_recv.at[q, u]).wait()


def chained(n, n_hid, n_rep, layer_input, query_weight, key_weight, value_weight, out_grad, doc_ids):
    m = n_hid * n_rep
    bf16, f32 = jnp.bfloat16, jnp.float32
    tok, feats = layer_input.shape
    total = tok * n
    rows = BLOCK
    count, per, piece = total // rows, tok // rows, rows // m
    q_cols = query_weight.shape[1]
    pair_width = key_weight.shape[1]
    width = q_cols // 2 + pair_width
    dma = pltpu.SemaphoreType.DMA
    ANY = pl.BlockSpec(memory_space=pl.ANY)
    turned, queries_all, pairs_all, input_grad = pl.pallas_call(
        functools.partial(chain_kernel, n, m, n_rep, rows, total // 2),
        out_shape=(
            jax.ShapeDtypeStruct((feats, total), bf16),
            jax.ShapeDtypeStruct((total, q_cols), bf16),
            jax.ShapeDtypeStruct((2, total, pair_width), bf16),
            jax.ShapeDtypeStruct((tok, feats), bf16),
        ),
        in_specs=[ANY] * 5 + [VM],
        out_specs=(ANY,) * 4,
        scratch_shapes=[
            pltpu.VMEM(query_weight.shape, bf16),
            pltpu.VMEM(key_weight.shape, bf16),
            pltpu.VMEM(value_weight.shape, bf16),
            pltpu.VMEM((total, feats), bf16),
            pltpu.VMEM((feats, total), bf16),
            pltpu.VMEM((total, q_cols), bf16),
            pltpu.VMEM((2, total, pair_width), bf16),
            pltpu.VMEM((2, total, width), bf16),
            pltpu.VMEM((2, total, width), bf16),
            pltpu.VMEM((total, q_cols // 2), bf16),
            pltpu.VMEM((total, DH), f32),
            pltpu.VMEM((total, DH), f32),
            pltpu.VMEM((2 * per, rows // 4, feats), bf16),
            pltpu.VMEM((total, feats), bf16),
            pltpu.VMEM((3, count * piece, feats), bf16),
            pltpu.VMEM((count * piece, feats), bf16),
            pltpu.VMEM((count * piece, feats), bf16),
            dma((2 * per,)), dma((2 * per,)), dma((2 * per, 2, 2)), dma((2 * count,)),
            dma((2 * count, 3)), dma((2 * count, 3)),
            dma((per, 2)), dma((count,)), dma((2, 2 * count)), dma((2, 2 * count)),
            dma((2, count)), dma((2, count)), dma((2, count)), dma((2, count)),
            dma((count, 3)), dma((count, 3)), dma((count,)), dma((m, per)), dma((count, 3)), dma((3,)),
        ],
        compiler_params=pltpu.CompilerParams(
            collective_id=0, has_side_effects=True, vmem_limit_bytes=VMEM_BYTES
        ),
    )(
        layer_input, out_grad, query_weight, key_weight, value_weight,
        doc_ids.reshape(1, total),
    )

    step = feats // n

    def whole(array):
        return pl.BlockSpec(array.shape, lambda i: (0,) * array.ndim)

    def part(rows, width):
        return pl.BlockSpec((rows, width), lambda i: (i, 0))

    weight_grads = pl.pallas_call(
        grad_kernel,
        grid=(n,),
        out_shape=(
            jax.ShapeDtypeStruct((tok, feats), bf16),
            jax.ShapeDtypeStruct((feats, q_cols), f32),
            jax.ShapeDtypeStruct((feats, pair_width), f32),
            jax.ShapeDtypeStruct((feats, pair_width), f32),
        ),
        in_specs=[part(step, total), whole(queries_all), whole(pairs_all), part(tok // n, feats)],
        out_specs=(
            part(tok // n, feats), part(step, q_cols), part(step, pair_width), part(step, pair_width)
        ),
        compiler_params=pltpu.CompilerParams(vmem_limit_bytes=VMEM_BYTES),
    )
    return weight_grads(turned, queries_all, pairs_all, input_grad)


def grad_kernel(xt_ref, dq_ref, kv_ref, in_ref, ig_ref, qg_ref, kg_ref, vg_ref):
    x = xt_ref[...]
    qg_ref[...] = jnp.dot(x, dq_ref[...], preferred_element_type=jnp.float32)
    kg_ref[...] = jnp.dot(x, kv_ref[0], preferred_element_type=jnp.float32)
    vg_ref[...] = jnp.dot(x, kv_ref[1], preferred_element_type=jnp.float32)
    ig_ref[...] = in_ref[...]


def solution(mesh):
    in_specs = (
        P(("groups", "srv"), ("hid", "rep")),
        P("srv", ("hid", "rep")),
        P("srv", ("hid", "rep")),
        P("srv", ("hid", "rep")),
        P(("groups", "srv"), ("hid", "rep")),
        P("groups"),
    )
    out_specs = (
        P(("groups", "srv"), ("hid", "rep")),
        P(("groups", "srv"), ("hid", "rep")),
        P(("groups", "srv"), ("hid", "rep")),
        P(("groups", "srv"), ("hid", "rep")),
    )
    n, n_hid, n_rep = mesh.shape["srv"], mesh.shape["hid"], mesh.shape["rep"]
    m = n_hid * n_rep
    inner = body
    if n == m and n_hid == 2 and n_rep == 2 and HK == 2 * m and HQ % HK == 0:
        inner = functools.partial(chained, n, n_hid, n_rep)
    return jax.shard_map(inner, mesh=mesh, in_specs=in_specs, out_specs=out_specs, check_vma=False)
```

```python
import functools

import jax
import jax.numpy as jnp
from jax import lax
from jax.experimental import pallas as pl
from jax.experimental.pallas import tpu as pltpu
from jax.sharding import PartitionSpec as P

HQ = 32
HK = 8
DH = 128
BLOCK = 128


NEGATIVE = -1e30


def attend(queries, cotangent, keys_all, values_all, doc_ids, block_id, carried):
    row_count = queries.shape[0]
    factor_scale = queries.shape[-1] ** (-0.5)
    offsets = jnp.arange(row_count, dtype=jnp.int32)
    query_pos = block_id * row_count + offsets
    query_doc = lax.dynamic_slice_in_dim(doc_ids, block_id * row_count, row_count)
    doc_start = jnp.sum((doc_ids < query_doc[0]).astype(jnp.int32))
    lowest = doc_start // row_count
    highest = jnp.where(True, block_id + 1, lowest)

    def scores_at(key_block):
        key_rows = lax.dynamic_slice_in_dim(keys_all, key_block * row_count, row_count, 0)
        value_rows = lax.dynamic_slice_in_dim(values_all, key_block * row_count, row_count, 0)
        key_doc = lax.dynamic_slice_in_dim(doc_ids, key_block * row_count, row_count)
        key_pos = key_block * row_count + offsets
        allowed = (key_doc[None, :] == query_doc[:, None]) & (
            key_pos[None, :] <= query_pos[:, None]
        )
        logits = (
            jnp.einsum("qgnd,kgd->gnqk", queries, key_rows, preferred_element_type=jnp.float32)
            * factor_scale
        )
        logits = jnp.where(allowed, logits, NEGATIVE)
        slopes = jnp.einsum(
            "qgnd,kgd->gnqk", cotangent, value_rows, preferred_element_type=jnp.float32
        )
        return (key_rows, allowed, logits, slopes)

    def first_pass(key_block, loop_state):
        row_peak, row_total, row_inner = loop_state
        key_rows, allowed, logits, slopes = scores_at(key_block)
        new_peak = jnp.maximum(row_peak, jnp.max(logits, axis=-1))
        weights = jnp.where(allowed, jnp.exp(logits - new_peak[..., None]), 0.0)
        factor = jnp.exp(row_peak - new_peak)
        row_total = row_total * factor + jnp.sum(weights, axis=-1)
        row_inner = row_inner * factor + jnp.sum(weights * slopes, axis=-1)
        return (new_peak, row_total, row_inner)

    stat_shape = (queries.shape[1], queries.shape[2], row_count)
    initial = (
        jnp.full(stat_shape, NEGATIVE, jnp.float32),
        jnp.zeros(stat_shape, jnp.float32),
        jnp.zeros(stat_shape, jnp.float32),
    )
    row_peak, row_total, row_inner = lax.fori_loop(lowest, highest, first_pass, initial)
    safe_total = jnp.where(True, row_total, 1.0)
    row_delta = row_inner / safe_total
    log_total = row_peak + jnp.log(safe_total)

    def second_pass(key_block, loop_state):
        query_grad, key_accum, value_accum = loop_state
        key_rows, allowed, logits, slopes = scores_at(key_block)
        attention = jnp.where(allowed, jnp.exp(logits - log_total[..., None]), 0.0)
        score_grad = (attention * (slopes - row_delta[..., None]) * factor_scale).astype(
            jnp.bfloat16
        )
        value_part = jnp.einsum(
            "gnqk,qgnd->kgd",
            attention.astype(jnp.bfloat16),
            cotangent,
            preferred_element_type=jnp.float32,
        )
        key_part = jnp.einsum(
            "gnqk,qgnd->kgd", score_grad, queries, preferred_element_type=jnp.float32
        )
        query_grad = query_grad + jnp.einsum(
            "gnqk,kgd->qgnd", score_grad, key_rows, preferred_element_type=jnp.float32
        )
        first_row = key_block * row_count
        key_accum = lax.dynamic_update_slice_in_dim(
            key_accum,
            lax.dynamic_slice_in_dim(key_accum, first_row, row_count, 0) + key_part,
            first_row,
            0,
        )
        value_accum = lax.dynamic_update_slice_in_dim(
            value_accum,
            lax.dynamic_slice_in_dim(value_accum, first_row, row_count, 0) + value_part,
            first_row,
            0,
        )
        return (query_grad, key_accum, value_accum)

    start_grad = jnp.zeros(queries.shape, jnp.float32)
    query_grad, key_accum, value_accum = lax.fori_loop(
        lowest, highest, second_pass, (start_grad, carried[0], carried[1])
    )
    return (query_grad, (key_accum, value_accum))


def body(layer_input, query_weight, key_weight, value_weight, out_grad, doc_ids):
    tok_rows = layer_input.shape[0]
    query_width = query_weight.shape[1]
    pair_width = key_weight.shape[1]
    key_heads = pair_width // DH
    group_size = HQ // HK
    block_count = tok_rows // BLOCK
    owner_id = lax.axis_index("srv")
    weights_all = lax.all_gather(
        jnp.concatenate([query_weight, key_weight, value_weight], axis=1), "srv", axis=0, tiled=True
    )
    inputs_all = lax.all_gather(layer_input, ("hid", "rep"), axis=1, tiled=True)
    projected = jnp.dot(inputs_all, weights_all, preferred_element_type=jnp.float32).astype(
        jnp.bfloat16
    )
    queries = projected[:, :query_width].reshape(block_count, BLOCK, key_heads, group_size, DH)
    keys_local = projected[:, query_width : query_width + pair_width]
    values_local = projected[:, query_width + pair_width :]
    keys_all, values_all = (
        lax.all_gather(keys_local, "srv", axis=0, tiled=True),
        lax.all_gather(values_local, "srv", axis=0, tiled=True),
    )
    total_rows = keys_all.shape[0]
    keys_all = keys_all.reshape(total_rows, key_heads, DH)
    values_all = values_all.reshape(total_rows, key_heads, DH)
    cotangent = out_grad.reshape(block_count, BLOCK, key_heads, group_size, DH)
    empty_accum = jnp.zeros((total_rows, key_heads, DH), jnp.float32)

    def own_block(position, loop_state):
        answers, carried = loop_state
        grad_q, carried = attend(
            lax.dynamic_index_in_dim(queries, position, 0, keepdims=False),
            lax.dynamic_index_in_dim(cotangent, position, 0, keepdims=False),
            keys_all,
            values_all,
            doc_ids,
            owner_id * block_count + position,
            carried,
        )
        answers = lax.dynamic_update_index_in_dim(answers, grad_q.astype(jnp.bfloat16), position, 0)
        return (answers, carried)

    answers = jnp.zeros(queries.shape, jnp.bfloat16)
    answers, carried = lax.fori_loop(
        0, block_count, own_block, (answers, (empty_accum, empty_accum))
    )
    query_grad = answers.reshape(tok_rows, query_width)
    key_accum, value_accum = carried
    key_sum, value_sum = (
        lax.psum_scatter(key_accum, "srv", scatter_dimension=0, tiled=True),
        lax.psum_scatter(value_accum, "srv", scatter_dimension=0, tiled=True),
    )
    grads_all = jnp.concatenate(
        [
            query_grad,
            key_sum.astype(jnp.bfloat16).reshape(tok_rows, pair_width),
            value_sum.astype(jnp.bfloat16).reshape(tok_rows, pair_width),
        ],
        axis=1,
    )
    input_terms = lax.dot_general(
        grads_all, weights_all, (((1,), (1,)), ((), ())), preferred_element_type=jnp.float32
    )
    input_grad = lax.psum_scatter(
        input_terms, ("hid", "rep"), scatter_dimension=1, tiled=True
    ).astype(jnp.bfloat16)
    columns = lax.all_to_all(inputs_all, "srv", split_axis=1, concat_axis=0, tiled=True)
    weight_grad = lax.dot_general(
        columns,
        lax.all_gather(grads_all, "srv", axis=0, tiled=True),
        (((0,), (0,)), ((), ())),
        preferred_element_type=jnp.float32,
    )
    return (
        input_grad,
        weight_grad[:, :query_width],
        weight_grad[:, query_width : query_width + pair_width],
        weight_grad[:, query_width + pair_width :],
    )


MESH = pl.DeviceIdType.MESH
VM = pl.BlockSpec(memory_space=pltpu.VMEM)
VMEM_BYTES = 60 * 1024 * 1024


def place(n_rep):
    return lax.axis_index("srv"), lax.axis_index("hid") * n_rep + lax.axis_index("rep")


def device_at(z, c, n_rep):
    return {"srv": z, "hid": c // n_rep, "rep": c % n_rep}


def greet(n, m, n_rep):
    z, c = place(n_rep)
    barrier = pltpu.get_barrier_semaphore()
    for dz in range(n):
        for dc in range(m):
            if dz or dc:
                pl.semaphore_signal(
                    barrier,
                    inc=1,
                    device_id=device_at((z + dz) % n, (c + dc) % m, n_rep),
                    device_id_type=MESH,
                )
    pl.semaphore_wait(barrier, n * m - 1)


def remote(src, dst, send, recv, device):
    return pltpu.make_async_remote_copy(
        src_ref=src, dst_ref=dst, send_sem=send, recv_sem=recv, device_id=device, device_id_type=MESH
    )


def rows_at(start, size):
    return pl.ds(pl.multiple_of(start, size), size)


def cols_at(start, size):
    return pl.ds(pl.multiple_of(start, DH), size)


def attend_rows(heads, qkv, og_ref, dc_ref, dq_ref, dq_cols, dk, dv, first, row_block, low, width):
    q_cols = heads * DH
    scale = DH ** (-0.5)
    rows = rows_at(first, row_block)
    span = rows_at(low, row_block) if width == row_block else pl.ds(pl.multiple_of(low, row_block), width)
    queries = jnp.concatenate([qkv[rows, h * DH : (h + 1) * DH] for h in range(heads)], axis=0)
    cotangent = jnp.concatenate([og_ref[rows, h * DH : (h + 1) * DH] for h in range(heads)], axis=0)
    keys = qkv[span, q_cols : q_cols + DH]
    values = qkv[span, q_cols + DH : q_cols + 2 * DH]
    row_pos = first + lax.broadcasted_iota(jnp.int32, (row_block, width), 0)
    key_pos = low + lax.broadcasted_iota(jnp.int32, (row_block, width), 1)
    row_doc = jnp.broadcast_to(dc_ref[:, rows].astype(jnp.float32), (row_block, row_block)).T[:, :1]
    kept = (row_doc == dc_ref[:, span].astype(jnp.float32)) & (key_pos <= row_pos)
    bias = jnp.concatenate([jnp.where(kept, 0.0, NEGATIVE)] * heads, axis=0)
    both = (((1,), (1,)), ((), ()))
    logits = lax.dot_general(queries, keys, both, preferred_element_type=jnp.float32) * scale + bias
    weights = jnp.exp(logits - jnp.max(logits, axis=1, keepdims=True))
    attention = weights * (1.0 / jnp.sum(weights, axis=1, keepdims=True))
    slopes = lax.dot_general(cotangent, values, both, preferred_element_type=jnp.float32)
    inner = jnp.sum(attention * slopes, axis=1, keepdims=True)
    score_grad = (attention * (slopes - inner) * scale).astype(jnp.bfloat16)
    down = (((0,), (0,)), ((), ()))
    query_grad = jnp.dot(score_grad, keys, preferred_element_type=jnp.float32).astype(jnp.bfloat16)
    for h in range(heads):
        dq_ref[rows, cols_at(dq_cols + h * DH, DH)] = query_grad[h * row_block : (h + 1) * row_block]
    dk[span, :] += lax.dot_general(score_grad, queries, down, preferred_element_type=jnp.float32)
    dv[span, :] += lax.dot_general(
        attention.astype(jnp.bfloat16), cotangent, down, preferred_element_type=jnp.float32
    )


def chain_kernel(
    n, m, n_rep, rows, longest,
    x_ref, og_ref, qw_in, kw_in, vw_in, dc_ref,
    turned_out, dqa_out, kva_out, ig_ref,
    qw_ref, kw_ref, vw_ref, cols_ref, turned, dqa_ref, kva_ref, rs_in, rs_out, og_own, dk, dv, hopped, early, terms, took, paired, done,
    h_send, h_recv, a_send, a_recv, b_send, b_recv, og_send, og_recv, rs_send, rs_recv,
    dq_send, dq_recv, kv_send, kv_recv, r_send, r_recv, e_send, e_recv, out_sem, w_sem,
):
    z, c = place(n_rep)
    tok, feats = x_ref.shape
    total = tok * n
    count = total // rows
    per = tok // rows
    piece = rows // m
    parts = tok // (rows // 2)
    share = rows // 4
    q_side = qw_ref.shape[1] // 2
    heads = q_side // DH
    delay = longest // rows
    lead = 5
    half = z // (n // 2)
    e = z * (1 - half) + (n - 1 - z) * half
    f = n - 1 - e
    inner = z + 1 - 2 * half
    outer = z - 1 + 2 * half
    side_b = half
    side_a = 1 - half
    near_end = (n - 1) * half
    far_end = (n - 1) * (1 - half)
    is_end = e == 0
    not_end = e > 0
    sibling = c + 1 - 2 * (c % 2)
    across = (c + 2) % m
    diagonal = across + 1 - 2 * (across % 2)
    sub = rows // 2
    f32, bf16 = jnp.float32, jnp.bfloat16

    def chunk_rows(j):
        return rows_at(j * rows, rows)

    def hop_copy(u):
        src = x_ref.at[rows_at(u * sub, sub)]
        return remote(src, hopped.at[u // 2], h_send, h_recv.at[u // 2], device_at(z, across, n_rep))

    def input_copy(u, i):
        p = (c // 2) * 2 + i
        plane = across if u % 2 else c
        if u % 2:
            src = hopped.at[u // 2, i * share : (i + 1) * share]
        else:
            src = x_ref.at[rows_at(u * sub + i * share, share)]
        dst = cols_ref.at[rows_at(z * tok + u * sub + i * share, share)]
        copy = remote(
            src, dst, a_send.at[u, i], a_recv.at[z * parts + u], device_at(plane, p, n_rep)
        )
        return (plane == z) & (p == c), src, dst, copy

    def send_input(u):
        for i in range(2):
            own, src, dst, copy = input_copy(u, i)

            @pl.when(own)
            def _():
                pltpu.make_async_copy(src, dst, a_recv.at[z * parts + u]).start()

            @pl.when(jnp.logical_not(own))
            def _():
                copy.start()

    def holds(g):
        return (c // 2 + z // (n // 2) + g) % 2 == 0

    def half_block(g):
        return cols_ref.at[rows_at(g * sub + (c % 2) * share, share)]

    def spread_copy(g, slot):
        block = half_block(g)
        return remote(
            block, block, b_send, b_recv.at[g, slot % 2],
            device_at(z, across if slot == 1 else sibling, n_rep),
        )

    def og_copy(u, s, slot, to):
        src = og_ref.at[rows_at(u * rows, rows), cols_at(s * q_side, q_side)]
        dst = og_own.at[chunk_rows(z * per + u)]
        return src, dst, remote(
            src, dst, og_send.at[u, slot], og_recv.at[z * per + u], device_at(to, c, n_rep)
        )

    def sub_rows(g):
        return rows_at(g * sub, sub)

    def rs_copy(s, g, to):
        return remote(
            rs_out.at[s, sub_rows(g)], rs_in.at[s, sub_rows(g)],
            rs_send.at[s], rs_recv.at[s, g], device_at(to, c, n_rep),
        )

    def dq_copy(s, j, to):
        block = dqa_ref.at[chunk_rows(j), cols_at(s * q_side, q_side)]
        return remote(block, block, dq_send.at[s], dq_recv.at[s, j], device_at(to, c, n_rep))

    def kv_copy(s, j, to):
        block = kva_ref.at[:, chunk_rows(j), cols_at(s * DH, DH)]
        return remote(block, block, kv_send.at[s], kv_recv.at[s, j], device_at(to, c, n_rep))

    def term_rows(j, owner):
        return rows_at(j * rows + owner * piece, piece)

    def term_copy(j, slot):
        return remote(
            terms.at[term_rows(j, diagonal if slot else sibling)],
            took.at[slot, rows_at(j * piece, piece)],
            r_send.at[0], r_recv.at[j, slot], device_at(z, sibling, n_rep),
        )

    def pair_copy(j):
        block = rows_at(j * piece, piece)
        return remote(
            paired.at[block], took.at[2, block],
            r_send.at[1], r_recv.at[j, 2], device_at(z, across, n_rep),
        )

    def done_place(j):
        return ig_ref.at[rows_at((j % per) * rows + c * piece, piece)]

    def done_copy(j):
        return remote(
            done.at[rows_at(j * piece, piece)], done_place(j),
            e_send.at[j], e_recv.at[c, j % per], device_at(j // per, z, n_rep),
        )

    def spread(g):
        @pl.when(holds(g))
        def _():
            block = half_block(g)
            pltpu.make_async_copy(block, block, a_recv.at[g]).wait()
            for slot in (1, 0):
                spread_copy(g, slot).start()

    def relay(g):
        @pl.when(jnp.logical_not(holds(g)))
        def _():
            spread_copy(g, 1).wait_recv()
            spread_copy(g, 2).start()

    def await_input(g):
        @pl.when(holds(g))
        def _():
            spread_copy(g, 0).wait_recv()

        @pl.when(jnp.logical_not(holds(g)))
        def _():
            spread_copy(g, 2).wait_recv()

    def project(s, g):
        x = cols_ref[sub_rows(g), :]
        return jnp.concatenate(
            [
                jnp.dot(x, qw_ref[:, cols_at(s * q_side, q_side)], preferred_element_type=f32),
                jnp.dot(x, kw_ref[:, cols_at(s * DH, DH)], preferred_element_type=f32),
                jnp.dot(x, vw_ref[:, cols_at(s * DH, DH)], preferred_element_type=f32),
            ],
            axis=1,
        )

    def add_in(s, g):
        part = project(s, g)
        rs_copy(s, g, inner).wait_recv()
        rs_out[s, sub_rows(g), :] = (part + rs_in[s, sub_rows(g), :].astype(f32)).astype(bf16)

    def out_copy(j, slot):
        if slot == 2:
            src, dst = kva_ref.at[:, chunk_rows(j)], kva_out.at[:, chunk_rows(j)]
        elif slot == 1:
            src, dst = dqa_ref.at[chunk_rows(j)], dqa_out.at[chunk_rows(j)]
        else:
            src, dst = turned.at[:, chunk_rows(j)], turned_out.at[:, chunk_rows(j)]
        return pltpu.make_async_copy(src, dst, out_sem.at[slot])

    def reduce_a(g):
        await_input(g)

        @pl.when(is_end)
        def _():
            rs_out[side_a, sub_rows(g), :] = project(side_a, g).astype(bf16)

        @pl.when(not_end)
        def _():
            add_in(side_a, g)

        rs_copy(side_a, g, inner).start()

    def reduce_b(g):
        add_in(side_b, g)

        @pl.when(not_end)
        def _():
            rs_copy(side_b, g, outer).start()

    def settle(i):
        kva_ref[0, chunk_rows(i), cols_at(side_b * DH, DH)] = dk[chunk_rows(i), :].astype(bf16)
        kva_ref[1, chunk_rows(i), cols_at(side_b * DH, DH)] = dv[chunk_rows(i), :].astype(bf16)
        kv_copy(side_b, i, inner).start()

    def attend_chunk(j):
        block = og_own.at[chunk_rows(j)]
        pltpu.make_async_copy(block, block, og_recv.at[j]).wait()
        run = functools.partial(
            attend_rows, heads, rs_out.at[side_b], og_own, dc_ref, dqa_ref, side_b * q_side, dk, dv
        )
        for b in range(delay):
            @pl.when(j == b)
            def _():
                run(b * rows, rows, 0, (b + 1) * rows)

        @pl.when(j >= delay)
        def _():
            run(j * rows, rows, (j - delay) * rows, (delay + 1) * rows)

        dq_copy(side_b, j, inner).start()

        @pl.when(j >= delay)
        def _():
            settle(j - delay)

        @pl.when(j == count - 1)
        def _():
            def rest(i, carry):
                settle(i)
                return carry

            lax.fori_loop(count - delay, count, rest, 0)

    def combine(j):
        term_copy(j, 1).wait_recv()
        block = rows_at(j * piece, piece)
        value = terms[term_rows(j, across), :].astype(f32) + took[1, block, :].astype(f32)
        paired[block, :] = value.astype(bf16)
        pair_copy(j).start()

    def finish(j):
        block = rows_at(j * piece, piece)
        term_copy(j, 0).wait_recv()
        value = terms[term_rows(j, c), :].astype(f32) + took[0, block, :].astype(f32)
        pair_copy(j).wait_recv()
        value = value + took[2, block, :].astype(f32)
        done[rows_at(j * piece, piece), :] = value.astype(bf16)
        own = (j // per == z) & (c == z)

        @pl.when(own)
        def _():
            pltpu.make_async_copy(
                done.at[rows_at(j * piece, piece)], done_place(j), e_recv.at[c, j % per]
            ).start()

        @pl.when(jnp.logical_not(own))
        def _():
            done_copy(j).start()

    def term(j):
        for slot in (1, 2):
            out_copy(j, slot).start()
        flip = (((1,), (1,)), ((), ()))
        value = early[chunk_rows(j), :]
        value = value + lax.dot_general(
            kva_ref[0, chunk_rows(j), :], kw_ref[...], flip, preferred_element_type=f32
        )
        value = value + lax.dot_general(
            kva_ref[1, chunk_rows(j), :], vw_ref[...], flip, preferred_element_type=f32
        )
        terms[chunk_rows(j), :] = value.astype(bf16)
        for slot in (1, 0):
            term_copy(j, slot).start()

        @pl.when(j > 1)
        def _():
            combine(j - 2)

    def pass_b(v):
        @pl.when(v < count)
        def _():
            dq_copy(side_b, v, inner).wait_recv()
            dq_copy(side_b, v, inner).start()

        @pl.when(v >= delay)
        def _():
            kv_copy(side_b, v - delay, inner).wait_recv()
            kv_copy(side_b, v - delay, inner).start()

    def pass_a(v):
        @pl.when(v < count)
        def _():
            dq_copy(side_a, v, inner).wait_recv()

            @pl.when(not_end)
            def _():
                dq_copy(side_a, v, outer).start()

            early[chunk_rows(v), :] = lax.dot_general(
                dqa_ref[chunk_rows(v), :], qw_ref[...], (((1,), (1,)), ((), ())),
                preferred_element_type=f32,
            )

        @pl.when(v >= delay)
        def _():
            kv_copy(side_a, v - delay, inner).wait_recv()

            @pl.when(not_end)
            def _():
                kv_copy(side_a, v - delay, outer).start()

            term(v - delay)

    loads = [
        pltpu.make_async_copy(qw_in, qw_ref, w_sem.at[0]),
        pltpu.make_async_copy(kw_in, kw_ref, w_sem.at[1]),
        pltpu.make_async_copy(vw_in, vw_ref, w_sem.at[2]),
    ]
    for copy in loads:
        copy.start()
    greet(n, m, n_rep)
    send_input(0)
    @pl.when(is_end)
    def _():
        dk[...] = jnp.zeros_like(dk)
        dv[...] = jnp.zeros_like(dv)

    def forward(u):
        hop_copy(u).wait_recv()
        send_input(u)

    def send_og(u, slot):
        to = (far_end, near_end)[slot]
        src, dst, copy = og_copy(u, (side_a, side_b)[slot], slot, to)
        if slot == 0:
            copy.start()
        else:
            @pl.when(is_end)
            def _():
                pltpu.make_async_copy(src, dst, og_recv.at[z * per + u]).start()

            @pl.when(not_end)
            def _():
                copy.start()

    def begin():
        for u in range(1, lead):
            if u < parts and u % 2:
                forward(u)
            spread(u)
        relay(1)
        for u in range(per):
            send_og(u, 1)

    spread(0)
    for u in range(1, parts, 2):
        hop_copy(u).start()
    for u in range(2, parts, 2):
        send_input(u)
    for copy in loads:
        copy.wait()
    relay(0)

    def step(k, carry):
        even = k % 2 == 0
        j = k // 2

        @pl.when((k % 2 == 1) & (j >= z * per) & (j < z * per + per))
        def _():
            send_og(j - z * per, 0)

        @pl.when((k > 0) & (k + 1 < 2 * count))
        def _():
            relay(k + 1)

        @pl.when((k >= 2 * e) & (k < 2 * e + 2 * count))
        def _():
            reduce_a(k - 2 * e)

        @pl.when(k == 0)
        def _():
            begin()

        @pl.when(k + lead < 2 * count)
        def _():
            spread(k + lead)

        @pl.when((k % 2 == 1) & (k >= 2 * e) & (k < 2 * e + 2 * count))
        def _():
            turned[:, chunk_rows(j - e)] = cols_ref[chunk_rows(j - e), :].T
            out_copy(j - e, 0).start()

        @pl.when((k >= 2 * f) & (k < 2 * f + 2 * count))
        def _():
            reduce_b(k - 2 * f)

        h = j + 1

        @pl.when(is_end & (k % 2 == 1) & (h >= n) & (h < n + count))
        def _():
            attend_chunk(h - n)

        @pl.when(not_end & (k % 2 == 1) & (h >= n + e) & (h < n + e + count + delay))
        def _():
            pass_b(h - n - e)

        @pl.when((k % 2 == 1) & (h >= n + f) & (h < n + f + count + delay))
        def _():
            pass_a(h - n - f)

        return carry

    lax.fori_loop(0, 2 * (count + delay + 2 * (n - 1) + 1), step, 0)
    for j in (count - 2, count - 1):
        combine(jnp.int32(j))

    def close(j, carry):
        finish(j)
        return carry

    lax.fori_loop(0, count, close, 0)

    def settled(ref, sem):
        pltpu.make_async_copy(ref, ref, sem).wait()

    def drain(j, carry):
        @pl.when(jnp.logical_not((j // per == z) & (c == z)))
        def _():
            done_copy(j).wait_send()

        return carry

    settled(cols_ref.at[: 3 * total // m], b_send)
    settled(terms.at[: 2 * total // m], r_send.at[0])
    settled(paired, r_send.at[1])
    settled(turned, out_sem.at[0])
    settled(dqa_ref, out_sem.at[1])
    settled(kva_ref, out_sem.at[2])
    settled(rs_out.at[side_a], rs_send.at[side_a])
    settled(og_own, dq_send.at[side_b])
    settled(kva_ref.at[side_b], kv_send.at[side_b])

    @pl.when(not_end)
    def _():
        settled(rs_out.at[side_b], rs_send.at[side_b])
        settled(og_own, dq_send.at[side_a])
        settled(kva_ref.at[side_a], kv_send.at[side_a])

    lax.fori_loop(0, count, drain, 0)
    settled(hopped, h_send)
    for u in range(parts):
        for i in range(2):
            own, _, _, copy = input_copy(u, i)

            @pl.when(jnp.logical_not(own))
            def _():
                copy.wait_send()
    for u in range(per):
        _, _, copy = og_copy(u, side_a, 0, far_end)
        copy.wait_send()

        @pl.when(not_end)
        def _():
            _, _, copy = og_copy(u, side_b, 1, near_end)
            copy.wait_send()

        for q in range(m):
            block = ig_ref.at[u * rows + q * piece : u * rows + (q + 1) * piece]
            pltpu.make_async_copy(block, block, e_recv.at[q, u]).wait()


def chained(n, n_hid, n_rep, layer_input, query_weight, key_weight, value_weight, out_grad, doc_ids):
    m = n_hid * n_rep
    bf16, f32 = jnp.bfloat16, jnp.float32
    tok, feats = layer_input.shape
    total = tok * n
    rows = BLOCK
    count, per, piece = total // rows, tok // rows, rows // m
    q_cols = query_weight.shape[1]
    pair_width = key_weight.shape[1]
    width = q_cols // 2 + pair_width
    dma = pltpu.SemaphoreType.DMA
    ANY = pl.BlockSpec(memory_space=pl.ANY)
    turned, queries_all, pairs_all, input_grad = pl.pallas_call(
        functools.partial(chain_kernel, n, m, n_rep, rows, total // 2),
        out_shape=(
            jax.ShapeDtypeStruct((feats, total), bf16),
            jax.ShapeDtypeStruct((total, q_cols), bf16),
            jax.ShapeDtypeStruct((2, total, pair_width), bf16),
            jax.ShapeDtypeStruct((tok, feats), bf16),
        ),
        in_specs=[ANY] * 5 + [VM],
        out_specs=(ANY,) * 4,
        scratch_shapes=[
            pltpu.VMEM(query_weight.shape, bf16),
            pltpu.VMEM(key_weight.shape, bf16),
            pltpu.VMEM(value_weight.shape, bf16),
            pltpu.VMEM((total, feats), bf16),
            pltpu.VMEM((feats, total), bf16),
            pltpu.VMEM((total, q_cols), bf16),
            pltpu.VMEM((2, total, pair_width), bf16),
            pltpu.VMEM((2, total, width), bf16),
            pltpu.VMEM((2, total, width), bf16),
            pltpu.VMEM((total, q_cols // 2), bf16),
            pltpu.VMEM((total, DH), f32),
            pltpu.VMEM((total, DH), f32),
            pltpu.VMEM((per, rows // 2, feats), bf16),
            pltpu.VMEM((total, feats), f32),
            pltpu.VMEM((total, feats), bf16),
            pltpu.VMEM((3, count * piece, feats), bf16),
            pltpu.VMEM((count * piece, feats), bf16),
            pltpu.VMEM((count * piece, feats), bf16),
            dma, dma((per,)), dma((2 * per, 2)), dma((2 * count,)),
            dma, dma((2 * count, 2)),
            dma((per, 2)), dma((count,)), dma((2,)), dma((2, 2 * count)),
            dma((2,)), dma((2, count)), dma((2,)), dma((2, count)),
            dma((2,)), dma((count, 3)), dma((count,)), dma((m, per)), dma((3,)), dma((3,)),
        ],
        compiler_params=pltpu.CompilerParams(
            collective_id=0, has_side_effects=True, vmem_limit_bytes=VMEM_BYTES
        ),
    )(
        layer_input, out_grad, query_weight, key_weight, value_weight,
        doc_ids.reshape(1, total),
    )

    step = feats // n

    def whole(array):
        return pl.BlockSpec(array.shape, lambda i: (0,) * array.ndim)

    def part(rows, width):
        return pl.BlockSpec((rows, width), lambda i: (i, 0))

    weight_grads = pl.pallas_call(
        grad_kernel,
        grid=(n,),
        out_shape=(
            jax.ShapeDtypeStruct((tok, feats), bf16),
            jax.ShapeDtypeStruct((feats, q_cols), f32),
            jax.ShapeDtypeStruct((feats, pair_width), f32),
            jax.ShapeDtypeStruct((feats, pair_width), f32),
        ),
        in_specs=[part(step, total), whole(queries_all), whole(pairs_all), part(tok // n, feats)],
        out_specs=(
            part(tok // n, feats), part(step, q_cols), part(step, pair_width), part(step, pair_width)
        ),
        compiler_params=pltpu.CompilerParams(vmem_limit_bytes=VMEM_BYTES),
    )
    return weight_grads(turned, queries_all, pairs_all, input_grad)


def grad_kernel(xt_ref, dq_ref, kv_ref, in_ref, ig_ref, qg_ref, kg_ref, vg_ref):
    x = xt_ref[...]
    qg_ref[...] = jnp.dot(x, dq_ref[...], preferred_element_type=jnp.float32)
    kg_ref[...] = jnp.dot(x, kv_ref[0], preferred_element_type=jnp.float32)
    vg_ref[...] = jnp.dot(x, kv_ref[1], preferred_element_type=jnp.float32)
    ig_ref[...] = in_ref[...]


def solution(mesh):
    in_specs = (
        P(("groups", "srv"), ("hid", "rep")),
        P("srv", ("hid", "rep")),
        P("srv", ("hid", "rep")),
        P("srv", ("hid", "rep")),
        P(("groups", "srv"), ("hid", "rep")),
        P("groups"),
    )
    out_specs = (
        P(("groups", "srv"), ("hid", "rep")),
        P(("groups", "srv"), ("hid", "rep")),
        P(("groups", "srv"), ("hid", "rep")),
        P(("groups", "srv"), ("hid", "rep")),
    )
    n, n_hid, n_rep = mesh.shape["srv"], mesh.shape["hid"], mesh.shape["rep"]
    m = n_hid * n_rep
    inner = body
    if n == m and n_hid == 2 and n_rep == 2 and HK == 2 * m and HQ % HK == 0:
        inner = functools.partial(chained, n, n_hid, n_rep)
    return jax.shard_map(inner, mesh=mesh, in_specs=in_specs, out_specs=out_specs, check_vma=False)
```

```python
import functools

import jax
import jax.numpy as jnp
from jax import lax
from jax.experimental import pallas as pl
from jax.experimental.pallas import tpu as pltpu
from jax.sharding import PartitionSpec as P

HQ = 32
HK = 8
DH = 128
BLOCK = 128


NEGATIVE = -1e30


def attend(queries, cotangent, keys_all, values_all, doc_ids, block_id, carried):
    row_count = queries.shape[0]
    factor_scale = queries.shape[-1] ** (-0.5)
    offsets = jnp.arange(row_count, dtype=jnp.int32)
    query_pos = block_id * row_count + offsets
    query_doc = lax.dynamic_slice_in_dim(doc_ids, block_id * row_count, row_count)
    doc_start = jnp.sum((doc_ids < query_doc[0]).astype(jnp.int32))
    lowest = doc_start // row_count
    highest = jnp.where(True, block_id + 1, lowest)

    def scores_at(key_block):
        key_rows = lax.dynamic_slice_in_dim(keys_all, key_block * row_count, row_count, 0)
        value_rows = lax.dynamic_slice_in_dim(values_all, key_block * row_count, row_count, 0)
        key_doc = lax.dynamic_slice_in_dim(doc_ids, key_block * row_count, row_count)
        key_pos = key_block * row_count + offsets
        allowed = (key_doc[None, :] == query_doc[:, None]) & (
            key_pos[None, :] <= query_pos[:, None]
        )
        logits = (
            jnp.einsum("qgnd,kgd->gnqk", queries, key_rows, preferred_element_type=jnp.float32)
            * factor_scale
        )
        logits = jnp.where(allowed, logits, NEGATIVE)
        slopes = jnp.einsum(
            "qgnd,kgd->gnqk", cotangent, value_rows, preferred_element_type=jnp.float32
        )
        return (key_rows, allowed, logits, slopes)

    def first_pass(key_block, loop_state):
        row_peak, row_total, row_inner = loop_state
        key_rows, allowed, logits, slopes = scores_at(key_block)
        new_peak = jnp.maximum(row_peak, jnp.max(logits, axis=-1))
        weights = jnp.where(allowed, jnp.exp(logits - new_peak[..., None]), 0.0)
        factor = jnp.exp(row_peak - new_peak)
        row_total = row_total * factor + jnp.sum(weights, axis=-1)
        row_inner = row_inner * factor + jnp.sum(weights * slopes, axis=-1)
        return (new_peak, row_total, row_inner)

    stat_shape = (queries.shape[1], queries.shape[2], row_count)
    initial = (
        jnp.full(stat_shape, NEGATIVE, jnp.float32),
        jnp.zeros(stat_shape, jnp.float32),
        jnp.zeros(stat_shape, jnp.float32),
    )
    row_peak, row_total, row_inner = lax.fori_loop(lowest, highest, first_pass, initial)
    safe_total = jnp.where(True, row_total, 1.0)
    row_delta = row_inner / safe_total
    log_total = row_peak + jnp.log(safe_total)

    def second_pass(key_block, loop_state):
        query_grad, key_accum, value_accum = loop_state
        key_rows, allowed, logits, slopes = scores_at(key_block)
        attention = jnp.where(allowed, jnp.exp(logits - log_total[..., None]), 0.0)
        score_grad = (attention * (slopes - row_delta[..., None]) * factor_scale).astype(
            jnp.bfloat16
        )
        value_part = jnp.einsum(
            "gnqk,qgnd->kgd",
            attention.astype(jnp.bfloat16),
            cotangent,
            preferred_element_type=jnp.float32,
        )
        key_part = jnp.einsum(
            "gnqk,qgnd->kgd", score_grad, queries, preferred_element_type=jnp.float32
        )
        query_grad = query_grad + jnp.einsum(
            "gnqk,kgd->qgnd", score_grad, key_rows, preferred_element_type=jnp.float32
        )
        first_row = key_block * row_count
        key_accum = lax.dynamic_update_slice_in_dim(
            key_accum,
            lax.dynamic_slice_in_dim(key_accum, first_row, row_count, 0) + key_part,
            first_row,
            0,
        )
        value_accum = lax.dynamic_update_slice_in_dim(
            value_accum,
            lax.dynamic_slice_in_dim(value_accum, first_row, row_count, 0) + value_part,
            first_row,
            0,
        )
        return (query_grad, key_accum, value_accum)

    start_grad = jnp.zeros(queries.shape, jnp.float32)
    query_grad, key_accum, value_accum = lax.fori_loop(
        lowest, highest, second_pass, (start_grad, carried[0], carried[1])
    )
    return (query_grad, (key_accum, value_accum))


def body(layer_input, query_weight, key_weight, value_weight, out_grad, doc_ids):
    tok_rows = layer_input.shape[0]
    query_width = query_weight.shape[1]
    pair_width = key_weight.shape[1]
    key_heads = pair_width // DH
    group_size = HQ // HK
    block_count = tok_rows // BLOCK
    owner_id = lax.axis_index("srv")
    weights_all = lax.all_gather(
        jnp.concatenate([query_weight, key_weight, value_weight], axis=1), "srv", axis=0, tiled=True
    )
    inputs_all = lax.all_gather(layer_input, ("hid", "rep"), axis=1, tiled=True)
    projected = jnp.dot(inputs_all, weights_all, preferred_element_type=jnp.float32).astype(
        jnp.bfloat16
    )
    queries = projected[:, :query_width].reshape(block_count, BLOCK, key_heads, group_size, DH)
    keys_local = projected[:, query_width : query_width + pair_width]
    values_local = projected[:, query_width + pair_width :]
    keys_all, values_all = (
        lax.all_gather(keys_local, "srv", axis=0, tiled=True),
        lax.all_gather(values_local, "srv", axis=0, tiled=True),
    )
    total_rows = keys_all.shape[0]
    keys_all = keys_all.reshape(total_rows, key_heads, DH)
    values_all = values_all.reshape(total_rows, key_heads, DH)
    cotangent = out_grad.reshape(block_count, BLOCK, key_heads, group_size, DH)
    empty_accum = jnp.zeros((total_rows, key_heads, DH), jnp.float32)

    def own_block(position, loop_state):
        answers, carried = loop_state
        grad_q, carried = attend(
            lax.dynamic_index_in_dim(queries, position, 0, keepdims=False),
            lax.dynamic_index_in_dim(cotangent, position, 0, keepdims=False),
            keys_all,
            values_all,
            doc_ids,
            owner_id * block_count + position,
            carried,
        )
        answers = lax.dynamic_update_index_in_dim(answers, grad_q.astype(jnp.bfloat16), position, 0)
        return (answers, carried)

    answers = jnp.zeros(queries.shape, jnp.bfloat16)
    answers, carried = lax.fori_loop(
        0, block_count, own_block, (answers, (empty_accum, empty_accum))
    )
    query_grad = answers.reshape(tok_rows, query_width)
    key_accum, value_accum = carried
    key_sum, value_sum = (
        lax.psum_scatter(key_accum, "srv", scatter_dimension=0, tiled=True),
        lax.psum_scatter(value_accum, "srv", scatter_dimension=0, tiled=True),
    )
    grads_all = jnp.concatenate(
        [
            query_grad,
            key_sum.astype(jnp.bfloat16).reshape(tok_rows, pair_width),
            value_sum.astype(jnp.bfloat16).reshape(tok_rows, pair_width),
        ],
        axis=1,
    )
    input_terms = lax.dot_general(
        grads_all, weights_all, (((1,), (1,)), ((), ())), preferred_element_type=jnp.float32
    )
    input_grad = lax.psum_scatter(
        input_terms, ("hid", "rep"), scatter_dimension=1, tiled=True
    ).astype(jnp.bfloat16)
    columns = lax.all_to_all(inputs_all, "srv", split_axis=1, concat_axis=0, tiled=True)
    weight_grad = lax.dot_general(
        columns,
        lax.all_gather(grads_all, "srv", axis=0, tiled=True),
        (((0,), (0,)), ((), ())),
        preferred_element_type=jnp.float32,
    )
    return (
        input_grad,
        weight_grad[:, :query_width],
        weight_grad[:, query_width : query_width + pair_width],
        weight_grad[:, query_width + pair_width :],
    )


MESH = pl.DeviceIdType.MESH
VM = pl.BlockSpec(memory_space=pltpu.VMEM)
VMEM_BYTES = 60 * 1024 * 1024


def place(n_rep):
    return lax.axis_index("srv"), lax.axis_index("hid") * n_rep + lax.axis_index("rep")


def device_at(z, c, n_rep):
    return {"srv": z, "hid": c // n_rep, "rep": c % n_rep}


def greet(n, m, n_rep):
    z, c = place(n_rep)
    barrier = pltpu.get_barrier_semaphore()
    for dz in range(n):
        for dc in range(m):
            if dz or dc:
                pl.semaphore_signal(
                    barrier,
                    inc=1,
                    device_id=device_at((z + dz) % n, (c + dc) % m, n_rep),
                    device_id_type=MESH,
                )
    pl.semaphore_wait(barrier, n * m - 1)


def remote(src, dst, send, recv, device):
    return pltpu.make_async_remote_copy(
        src_ref=src, dst_ref=dst, send_sem=send, recv_sem=recv, device_id=device, device_id_type=MESH
    )


def rows_at(start, size):
    return pl.ds(pl.multiple_of(start, size), size)


def cols_at(start, size):
    return pl.ds(pl.multiple_of(start, DH), size)


def attend_rows(heads, qkv, og_ref, dc_ref, dq_ref, dq_cols, dk, dv, first, row_block, low, width):
    q_cols = heads * DH
    scale = DH ** (-0.5)
    rows = rows_at(first, row_block)
    span = rows_at(low, row_block) if width == row_block else pl.ds(pl.multiple_of(low, row_block), width)
    queries = jnp.concatenate([qkv[rows, h * DH : (h + 1) * DH] for h in range(heads)], axis=0)
    cotangent = jnp.concatenate([og_ref[rows, h * DH : (h + 1) * DH] for h in range(heads)], axis=0)
    keys = qkv[span, q_cols : q_cols + DH]
    values = qkv[span, q_cols + DH : q_cols + 2 * DH]
    row_pos = first + lax.broadcasted_iota(jnp.int32, (row_block, width), 0)
    key_pos = low + lax.broadcasted_iota(jnp.int32, (row_block, width), 1)
    row_doc = jnp.broadcast_to(dc_ref[:, rows].astype(jnp.float32), (row_block, row_block)).T[:, :1]
    kept = (row_doc == dc_ref[:, span].astype(jnp.float32)) & (key_pos <= row_pos)
    bias = jnp.concatenate([jnp.where(kept, 0.0, NEGATIVE)] * heads, axis=0)
    both = (((1,), (1,)), ((), ()))
    logits = lax.dot_general(queries, keys, both, preferred_element_type=jnp.float32) * scale + bias
    weights = jnp.exp(logits - jnp.max(logits, axis=1, keepdims=True))
    attention = weights * (1.0 / jnp.sum(weights, axis=1, keepdims=True))
    slopes = lax.dot_general(cotangent, values, both, preferred_element_type=jnp.float32)
    inner = jnp.sum(attention * slopes, axis=1, keepdims=True)
    score_grad = (attention * (slopes - inner) * scale).astype(jnp.bfloat16)
    down = (((0,), (0,)), ((), ()))
    query_grad = jnp.dot(score_grad, keys, preferred_element_type=jnp.float32).astype(jnp.bfloat16)
    for h in range(heads):
        dq_ref[rows, cols_at(dq_cols + h * DH, DH)] = query_grad[h * row_block : (h + 1) * row_block]
    dk[span, :] += lax.dot_general(score_grad, queries, down, preferred_element_type=jnp.float32)
    dv[span, :] += lax.dot_general(
        attention.astype(jnp.bfloat16), cotangent, down, preferred_element_type=jnp.float32
    )


def chain_kernel(
    n, m, n_rep, rows, longest,
    x_ref, og_ref, qw_in, kw_in, vw_in, dc_ref,
    turned_out, dqa_out, kva_out, ig_ref,
    qw_ref, kw_ref, vw_ref, cols_ref, turned, dqa_ref, kva_ref, rs_in, rs_out, og_own, dk, dv, hopped, early, terms, took, paired, done,
    h_send, h_recv, a_send, a_recv, b_send, b_recv, og_send, og_recv, rs_send, rs_recv,
    dq_send, dq_recv, kv_send, kv_recv, r_send, r_recv, e_send, e_recv, out_sem, w_sem,
):
    z, c = place(n_rep)
    tok, feats = x_ref.shape
    total = tok * n
    count = total // rows
    per = tok // rows
    piece = rows // m
    parts = tok // (rows // 2)
    share = rows // 4
    q_side = qw_ref.shape[1] // 2
    heads = q_side // DH
    delay = longest // rows
    lead = 5
    half = z // (n // 2)
    e = z * (1 - half) + (n - 1 - z) * half
    f = n - 1 - e
    inner = z + 1 - 2 * half
    outer = z - 1 + 2 * half
    side_b = half
    side_a = 1 - half
    near_end = (n - 1) * half
    far_end = (n - 1) * (1 - half)
    is_end = e == 0
    not_end = e > 0
    sibling = c + 1 - 2 * (c % 2)
    across = (c + 2) % m
    diagonal = across + 1 - 2 * (across % 2)
    sub = rows // 2
    f32, bf16 = jnp.float32, jnp.bfloat16

    def chunk_rows(j):
        return rows_at(j * rows, rows)

    def hop_copy(u):
        src = x_ref.at[rows_at(u * sub, sub)]
        return remote(src, hopped.at[u // 2], h_send, h_recv.at[u // 2], device_at(z, across, n_rep))

    def input_copy(u, i):
        p = (c // 2) * 2 + i
        plane = across if u % 2 else c
        if u % 2:
            src = hopped.at[u // 2, i * share : (i + 1) * share]
        else:
            src = x_ref.at[rows_at(u * sub + i * share, share)]
        dst = cols_ref.at[rows_at(z * tok + u * sub + i * share, share)]
        copy = remote(
            src, dst, a_send.at[u, i], a_recv.at[z * parts + u], device_at(plane, p, n_rep)
        )
        return (plane == z) & (p == c), src, dst, copy

    def send_input(u):
        for i in range(2):
            own, src, dst, copy = input_copy(u, i)

            @pl.when(own)
            def _():
                pltpu.make_async_copy(src, dst, a_recv.at[z * parts + u]).start()

            @pl.when(jnp.logical_not(own))
            def _():
                copy.start()

    def holds(g):
        return (c // 2 + z // (n // 2) + g) % 2 == 0

    def half_block(g):
        return cols_ref.at[rows_at(g * sub + (c % 2) * share, share)]

    def spread_copy(g, slot):
        block = half_block(g)
        return remote(
            block, block, b_send, b_recv.at[g, slot % 2],
            device_at(z, across if slot == 1 else sibling, n_rep),
        )

    def og_copy(u, s, slot, to):
        src = og_ref.at[rows_at(u * rows, rows), cols_at(s * q_side, q_side)]
        dst = og_own.at[chunk_rows(z * per + u)]
        return src, dst, remote(
            src, dst, og_send.at[u, slot], og_recv.at[z * per + u], device_at(to, c, n_rep)
        )

    def sub_rows(g):
        return rows_at(g * sub, sub)

    def rs_copy(s, g, to):
        return remote(
            rs_out.at[s, sub_rows(g)], rs_in.at[s, sub_rows(g)],
            rs_send.at[s], rs_recv.at[s, g], device_at(to, c, n_rep),
        )

    def dq_copy(s, j, to):
        block = dqa_ref.at[chunk_rows(j), cols_at(s * q_side, q_side)]
        return remote(block, block, dq_send.at[s], dq_recv.at[s, j], device_at(to, c, n_rep))

    def kv_copy(s, j, to):
        block = kva_ref.at[:, chunk_rows(j), cols_at(s * DH, DH)]
        return remote(block, block, kv_send.at[s], kv_recv.at[s, j], device_at(to, c, n_rep))

    def term_rows(j, owner):
        return rows_at(j * rows + owner * piece, piece)

    def term_copy(j, slot):
        return remote(
            terms.at[term_rows(j, diagonal if slot else sibling)],
            took.at[slot, rows_at(j * piece, piece)],
            r_send.at[0], r_recv.at[j, slot], device_at(z, sibling, n_rep),
        )

    def pair_copy(j):
        block = rows_at(j * piece, piece)
        return remote(
            paired.at[block], took.at[2, block],
            r_send.at[1], r_recv.at[j, 2], device_at(z, across, n_rep),
        )

    def done_place(j):
        return ig_ref.at[rows_at((j % per) * rows + c * piece, piece)]

    def done_copy(j):
        return remote(
            done.at[rows_at(j * piece, piece)], done_place(j),
            e_send.at[j], e_recv.at[c, j % per], device_at(j // per, z, n_rep),
        )

    def spread(g):
        @pl.when(holds(g))
        def _():
            block = half_block(g)
            pltpu.make_async_copy(block, block, a_recv.at[g]).wait()
            for slot in (1, 0):
                spread_copy(g, slot).start()

    def relay(g):
        @pl.when(jnp.logical_not(holds(g)))
        def _():
            spread_copy(g, 1).wait_recv()
            spread_copy(g, 2).start()

    def await_input(g):
        @pl.when(holds(g))
        def _():
            spread_copy(g, 0).wait_recv()

        @pl.when(jnp.logical_not(holds(g)))
        def _():
            spread_copy(g, 2).wait_recv()

    def project(s, g):
        x = cols_ref[sub_rows(g), :]
        return jnp.concatenate(
            [
                jnp.dot(x, qw_ref[:, cols_at(s * q_side, q_side)], preferred_element_type=f32),
                jnp.dot(x, kw_ref[:, cols_at(s * DH, DH)], preferred_element_type=f32),
                jnp.dot(x, vw_ref[:, cols_at(s * DH, DH)], preferred_element_type=f32),
            ],
            axis=1,
        )

    def add_in(s, g):
        part = project(s, g)
        rs_copy(s, g, inner).wait_recv()
        rs_out[s, sub_rows(g), :] = (part + rs_in[s, sub_rows(g), :].astype(f32)).astype(bf16)

    def out_copy(j, slot):
        if slot == 2:
            src, dst = kva_ref.at[:, chunk_rows(j)], kva_out.at[:, chunk_rows(j)]
        elif slot == 1:
            src, dst = dqa_ref.at[chunk_rows(j)], dqa_out.at[chunk_rows(j)]
        else:
            src, dst = turned.at[:, chunk_rows(j)], turned_out.at[:, chunk_rows(j)]
        return pltpu.make_async_copy(src, dst, out_sem.at[slot])

    def reduce_a(g):
        await_input(g)

        @pl.when(is_end)
        def _():
            rs_out[side_a, sub_rows(g), :] = project(side_a, g).astype(bf16)

        @pl.when(not_end)
        def _():
            add_in(side_a, g)

        rs_copy(side_a, g, inner).start()

    def reduce_b(g):
        add_in(side_b, g)

        @pl.when(not_end)
        def _():
            rs_copy(side_b, g, outer).start()

    def settle(i):
        kva_ref[0, chunk_rows(i), cols_at(side_b * DH, DH)] = dk[chunk_rows(i), :].astype(bf16)
        kva_ref[1, chunk_rows(i), cols_at(side_b * DH, DH)] = dv[chunk_rows(i), :].astype(bf16)
        kv_copy(side_b, i, inner).start()

    def attend_chunk(j):
        block = og_own.at[chunk_rows(j)]
        pltpu.make_async_copy(block, block, og_recv.at[j]).wait()
        run = functools.partial(
            attend_rows, heads, rs_out.at[side_b], og_own, dc_ref, dqa_ref, side_b * q_side, dk, dv
        )
        for b in range(delay):
            @pl.when(j == b)
            def _():
                run(b * rows, rows, 0, (b + 1) * rows)

        @pl.when(j >= delay)
        def _():
            run(j * rows, rows, (j - delay) * rows, (delay + 1) * rows)

        dq_copy(side_b, j, inner).start()

        @pl.when(j >= delay)
        def _():
            settle(j - delay)

        @pl.when(j == count - 1)
        def _():
            def rest(i, carry):
                settle(i)
                return carry

            lax.fori_loop(count - delay, count, rest, 0)

    def combine(j):
        term_copy(j, 1).wait_recv()
        block = rows_at(j * piece, piece)
        value = terms[term_rows(j, across), :].astype(f32) + took[1, block, :].astype(f32)
        paired[block, :] = value.astype(bf16)
        pair_copy(j).start()

    def finish(j):
        block = rows_at(j * piece, piece)
        term_copy(j, 0).wait_recv()
        value = terms[term_rows(j, c), :].astype(f32) + took[0, block, :].astype(f32)
        pair_copy(j).wait_recv()
        value = value + took[2, block, :].astype(f32)
        done[rows_at(j * piece, piece), :] = value.astype(bf16)
        own = (j // per == z) & (c == z)

        @pl.when(own)
        def _():
            pltpu.make_async_copy(
                done.at[rows_at(j * piece, piece)], done_place(j), e_recv.at[c, j % per]
            ).start()

        @pl.when(jnp.logical_not(own))
        def _():
            done_copy(j).start()

    def term(j):
        for slot in (1, 2):
            out_copy(j, slot).start()
        flip = (((1,), (1,)), ((), ()))
        value = early[chunk_rows(j), :]
        value = value + lax.dot_general(
            kva_ref[0, chunk_rows(j), :], kw_ref[...], flip, preferred_element_type=f32
        )
        value = value + lax.dot_general(
            kva_ref[1, chunk_rows(j), :], vw_ref[...], flip, preferred_element_type=f32
        )
        terms[chunk_rows(j), :] = value.astype(bf16)
        for slot in (1, 0):
            term_copy(j, slot).start()

        @pl.when(j > 0)
        def _():
            combine(j - 1)

    def pass_b(v):
        @pl.when(v < count)
        def _():
            dq_copy(side_b, v, inner).wait_recv()
            dq_copy(side_b, v, inner).start()

        @pl.when(v >= delay)
        def _():
            kv_copy(side_b, v - delay, inner).wait_recv()
            kv_copy(side_b, v - delay, inner).start()

    def pass_a(v):
        @pl.when(v < count)
        def _():
            dq_copy(side_a, v, inner).wait_recv()

            @pl.when(not_end)
            def _():
                dq_copy(side_a, v, outer).start()

            early[chunk_rows(v), :] = lax.dot_general(
                dqa_ref[chunk_rows(v), :], qw_ref[...], (((1,), (1,)), ((), ())),
                preferred_element_type=f32,
            )

        @pl.when(v >= delay)
        def _():
            kv_copy(side_a, v - delay, inner).wait_recv()

            @pl.when(not_end)
            def _():
                kv_copy(side_a, v - delay, outer).start()

            term(v - delay)

    loads = [
        pltpu.make_async_copy(qw_in, qw_ref, w_sem.at[0]),
        pltpu.make_async_copy(kw_in, kw_ref, w_sem.at[1]),
        pltpu.make_async_copy(vw_in, vw_ref, w_sem.at[2]),
    ]
    for copy in loads:
        copy.start()
    greet(n, m, n_rep)
    send_input(0)
    @pl.when(is_end)
    def _():
        dk[...] = jnp.zeros_like(dk)
        dv[...] = jnp.zeros_like(dv)

    def forward(u):
        hop_copy(u).wait_recv()
        send_input(u)

    def send_og(u, slot):
        to = (far_end, near_end)[slot]
        src, dst, copy = og_copy(u, (side_a, side_b)[slot], slot, to)
        if slot == 0:
            copy.start()
        else:
            @pl.when(is_end)
            def _():
                pltpu.make_async_copy(src, dst, og_recv.at[z * per + u]).start()

            @pl.when(not_end)
            def _():
                copy.start()

    def begin():
        for u in range(1, lead):
            if u < parts and u % 2:
                forward(u)
            spread(u)
        relay(1)
        for u in range(per):
            send_og(u, 1)

            send_og(u, 0)

    spread(0)
    for u in range(1, parts, 2):
        hop_copy(u).start()
    for u in range(2, parts, 2):
        send_input(u)
    for copy in loads:
        copy.wait()
    relay(0)

    def step(k, carry):
        even = k % 2 == 0
        j = k // 2


        @pl.when((k > 0) & (k + 1 < 2 * count))
        def _():
            relay(k + 1)

        @pl.when((k >= 2 * e) & (k < 2 * e + 2 * count))
        def _():
            reduce_a(k - 2 * e)

        @pl.when(k == 0)
        def _():
            begin()

        @pl.when(k + lead < 2 * count)
        def _():
            spread(k + lead)

        @pl.when((k % 2 == 1) & (k >= 2 * e) & (k < 2 * e + 2 * count))
        def _():
            turned[:, chunk_rows(j - e)] = cols_ref[chunk_rows(j - e), :].T
            out_copy(j - e, 0).start()

        @pl.when((k >= 2 * f) & (k < 2 * f + 2 * count))
        def _():
            reduce_b(k - 2 * f)

        h = j + 1

        @pl.when(is_end & (k % 2 == 1) & (h >= n) & (h < n + count))
        def _():
            attend_chunk(h - n)

        @pl.when(not_end & (k % 2 == 1) & (h >= n + e) & (h < n + e + count + delay))
        def _():
            pass_b(h - n - e)

        @pl.when((k % 2 == 1) & (h >= n + f) & (h < n + f + count + delay))
        def _():
            pass_a(h - n - f)

        return carry

    lax.fori_loop(0, 2 * (count + delay + 2 * (n - 1) + 1), step, 0)
    for j in (count - 1,):
        combine(jnp.int32(j))

    def close(j, carry):
        finish(j)
        return carry

    lax.fori_loop(0, count, close, 0)

    def settled(ref, sem):
        pltpu.make_async_copy(ref, ref, sem).wait()

    def drain(j, carry):
        @pl.when(jnp.logical_not((j // per == z) & (c == z)))
        def _():
            done_copy(j).wait_send()

        return carry

    settled(cols_ref.at[: 3 * total // m], b_send)
    settled(terms.at[: 2 * total // m], r_send.at[0])
    settled(paired, r_send.at[1])
    settled(turned, out_sem.at[0])
    settled(dqa_ref, out_sem.at[1])
    settled(kva_ref, out_sem.at[2])
    settled(rs_out.at[side_a], rs_send.at[side_a])
    settled(og_own, dq_send.at[side_b])
    settled(kva_ref.at[side_b], kv_send.at[side_b])

    @pl.when(not_end)
    def _():
        settled(rs_out.at[side_b], rs_send.at[side_b])
        settled(og_own, dq_send.at[side_a])
        settled(kva_ref.at[side_a], kv_send.at[side_a])

    lax.fori_loop(0, count, drain, 0)
    settled(hopped, h_send)
    for u in range(parts):
        for i in range(2):
            own, _, _, copy = input_copy(u, i)

            @pl.when(jnp.logical_not(own))
            def _():
                copy.wait_send()
    for u in range(per):
        _, _, copy = og_copy(u, side_a, 0, far_end)
        copy.wait_send()

        @pl.when(not_end)
        def _():
            _, _, copy = og_copy(u, side_b, 1, near_end)
            copy.wait_send()

        for q in range(m):
            block = ig_ref.at[u * rows + q * piece : u * rows + (q + 1) * piece]
            pltpu.make_async_copy(block, block, e_recv.at[q, u]).wait()


def chained(n, n_hid, n_rep, layer_input, query_weight, key_weight, value_weight, out_grad, doc_ids):
    m = n_hid * n_rep
    bf16, f32 = jnp.bfloat16, jnp.float32
    tok, feats = layer_input.shape
    total = tok * n
    rows = BLOCK
    count, per, piece = total // rows, tok // rows, rows // m
    q_cols = query_weight.shape[1]
    pair_width = key_weight.shape[1]
    width = q_cols // 2 + pair_width
    dma = pltpu.SemaphoreType.DMA
    ANY = pl.BlockSpec(memory_space=pl.ANY)
    turned, queries_all, pairs_all, input_grad = pl.pallas_call(
        functools.partial(chain_kernel, n, m, n_rep, rows, total // 2),
        out_shape=(
            jax.ShapeDtypeStruct((feats, total), bf16),
            jax.ShapeDtypeStruct((total, q_cols), bf16),
            jax.ShapeDtypeStruct((2, total, pair_width), bf16),
            jax.ShapeDtypeStruct((tok, feats), bf16),
        ),
        in_specs=[ANY] * 5 + [VM],
        out_specs=(ANY,) * 4,
        scratch_shapes=[
            pltpu.VMEM(query_weight.shape, bf16),
            pltpu.VMEM(key_weight.shape, bf16),
            pltpu.VMEM(value_weight.shape, bf16),
            pltpu.VMEM((total, feats), bf16),
            pltpu.VMEM((feats, total), bf16),
            pltpu.VMEM((total, q_cols), bf16),
            pltpu.VMEM((2, total, pair_width), bf16),
            pltpu.VMEM((2, total, width), bf16),
            pltpu.VMEM((2, total, width), bf16),
            pltpu.VMEM((total, q_cols // 2), bf16),
            pltpu.VMEM((total, DH), f32),
            pltpu.VMEM((total, DH), f32),
            pltpu.VMEM((per, rows // 2, feats), bf16),
            pltpu.VMEM((total, feats), f32),
            pltpu.VMEM((total, feats), bf16),
            pltpu.VMEM((3, count * piece, feats), bf16),
            pltpu.VMEM((count * piece, feats), bf16),
            pltpu.VMEM((count * piece, feats), bf16),
            dma, dma((per,)), dma((2 * per, 2)), dma((2 * count,)),
            dma, dma((2 * count, 2)),
            dma((per, 2)), dma((count,)), dma((2,)), dma((2, 2 * count)),
            dma((2,)), dma((2, count)), dma((2,)), dma((2, count)),
            dma((2,)), dma((count, 3)), dma((count,)), dma((m, per)), dma((3,)), dma((3,)),
        ],
        compiler_params=pltpu.CompilerParams(
            collective_id=0, has_side_effects=True, vmem_limit_bytes=VMEM_BYTES
        ),
    )(
        layer_input, out_grad, query_weight, key_weight, value_weight,
        doc_ids.reshape(1, total),
    )

    blocks = n // 2
    step = feats // blocks

    def whole(array):
        return pl.BlockSpec(array.shape, lambda i: (0,) * array.ndim)

    def part(rows, width):
        return pl.BlockSpec((rows, width), lambda i: (i, 0))

    weight_grads = pl.pallas_call(
        grad_kernel,
        grid=(blocks,),
        out_shape=(
            jax.ShapeDtypeStruct((tok, feats), bf16),
            jax.ShapeDtypeStruct((feats, q_cols), f32),
            jax.ShapeDtypeStruct((feats, pair_width), f32),
            jax.ShapeDtypeStruct((feats, pair_width), f32),
        ),
        in_specs=[part(step, total), whole(queries_all), whole(pairs_all), part(tok // blocks, feats)],
        out_specs=(
            part(tok // blocks, feats), part(step, q_cols), part(step, pair_width), part(step, pair_width)
        ),
        compiler_params=pltpu.CompilerParams(vmem_limit_bytes=VMEM_BYTES),
    )
    return weight_grads(turned, queries_all, pairs_all, input_grad)


def grad_kernel(xt_ref, dq_ref, kv_ref, in_ref, ig_ref, qg_ref, kg_ref, vg_ref):
    x = xt_ref[...]
    qg_ref[...] = jnp.dot(x, dq_ref[...], preferred_element_type=jnp.float32)
    kg_ref[...] = jnp.dot(x, kv_ref[0], preferred_element_type=jnp.float32)
    vg_ref[...] = jnp.dot(x, kv_ref[1], preferred_element_type=jnp.float32)
    ig_ref[...] = in_ref[...]


def solution(mesh):
    in_specs = (
        P(("groups", "srv"), ("hid", "rep")),
        P("srv", ("hid", "rep")),
        P("srv", ("hid", "rep")),
        P("srv", ("hid", "rep")),
        P(("groups", "srv"), ("hid", "rep")),
        P("groups"),
    )
    out_specs = (
        P(("groups", "srv"), ("hid", "rep")),
        P(("groups", "srv"), ("hid", "rep")),
        P(("groups", "srv"), ("hid", "rep")),
        P(("groups", "srv"), ("hid", "rep")),
    )
    n, n_hid, n_rep = mesh.shape["srv"], mesh.shape["hid"], mesh.shape["rep"]
    m = n_hid * n_rep
    inner = body
    if n == m and n_hid == 2 and n_rep == 2 and HK == 2 * m and HQ % HK == 0:
        inner = functools.partial(chained, n, n_hid, n_rep)
    return jax.shard_map(inner, mesh=mesh, in_specs=in_specs, out_specs=out_specs, check_vma=False)
```

```python
import functools

import jax
import jax.numpy as jnp
from jax import lax
from jax.experimental import pallas as pl
from jax.experimental.pallas import tpu as pltpu
from jax.sharding import PartitionSpec as P

HQ = 32
HK = 8
DH = 128
BLOCK = 128


NEGATIVE = -1e30


def attend(queries, cotangent, keys_all, values_all, doc_ids, block_id, carried):
    row_count = queries.shape[0]
    factor_scale = queries.shape[-1] ** (-0.5)
    offsets = jnp.arange(row_count, dtype=jnp.int32)
    query_pos = block_id * row_count + offsets
    query_doc = lax.dynamic_slice_in_dim(doc_ids, block_id * row_count, row_count)
    doc_start = jnp.sum((doc_ids < query_doc[0]).astype(jnp.int32))
    lowest = doc_start // row_count
    highest = jnp.where(True, block_id + 1, lowest)

    def scores_at(key_block):
        key_rows = lax.dynamic_slice_in_dim(keys_all, key_block * row_count, row_count, 0)
        value_rows = lax.dynamic_slice_in_dim(values_all, key_block * row_count, row_count, 0)
        key_doc = lax.dynamic_slice_in_dim(doc_ids, key_block * row_count, row_count)
        key_pos = key_block * row_count + offsets
        allowed = (key_doc[None, :] == query_doc[:, None]) & (
            key_pos[None, :] <= query_pos[:, None]
        )
        logits = (
            jnp.einsum("qgnd,kgd->gnqk", queries, key_rows, preferred_element_type=jnp.float32)
            * factor_scale
        )
        logits = jnp.where(allowed, logits, NEGATIVE)
        slopes = jnp.einsum(
            "qgnd,kgd->gnqk", cotangent, value_rows, preferred_element_type=jnp.float32
        )
        return (key_rows, allowed, logits, slopes)

    def first_pass(key_block, loop_state):
        row_peak, row_total, row_inner = loop_state
        key_rows, allowed, logits, slopes = scores_at(key_block)
        new_peak = jnp.maximum(row_peak, jnp.max(logits, axis=-1))
        weights = jnp.where(allowed, jnp.exp(logits - new_peak[..., None]), 0.0)
        factor = jnp.exp(row_peak - new_peak)
        row_total = row_total * factor + jnp.sum(weights, axis=-1)
        row_inner = row_inner * factor + jnp.sum(weights * slopes, axis=-1)
        return (new_peak, row_total, row_inner)

    stat_shape = (queries.shape[1], queries.shape[2], row_count)
    initial = (
        jnp.full(stat_shape, NEGATIVE, jnp.float32),
        jnp.zeros(stat_shape, jnp.float32),
        jnp.zeros(stat_shape, jnp.float32),
    )
    row_peak, row_total, row_inner = lax.fori_loop(lowest, highest, first_pass, initial)
    safe_total = jnp.where(True, row_total, 1.0)
    row_delta = row_inner / safe_total
    log_total = row_peak + jnp.log(safe_total)

    def second_pass(key_block, loop_state):
        query_grad, key_accum, value_accum = loop_state
        key_rows, allowed, logits, slopes = scores_at(key_block)
        attention = jnp.where(allowed, jnp.exp(logits - log_total[..., None]), 0.0)
        score_grad = (attention * (slopes - row_delta[..., None]) * factor_scale).astype(
            jnp.bfloat16
        )
        value_part = jnp.einsum(
            "gnqk,qgnd->kgd",
            attention.astype(jnp.bfloat16),
            cotangent,
            preferred_element_type=jnp.float32,
        )
        key_part = jnp.einsum(
            "gnqk,qgnd->kgd", score_grad, queries, preferred_element_type=jnp.float32
        )
        query_grad = query_grad + jnp.einsum(
            "gnqk,kgd->qgnd", score_grad, key_rows, preferred_element_type=jnp.float32
        )
        first_row = key_block * row_count
        key_accum = lax.dynamic_update_slice_in_dim(
            key_accum,
            lax.dynamic_slice_in_dim(key_accum, first_row, row_count, 0) + key_part,
            first_row,
            0,
        )
        value_accum = lax.dynamic_update_slice_in_dim(
            value_accum,
            lax.dynamic_slice_in_dim(value_accum, first_row, row_count, 0) + value_part,
            first_row,
            0,
        )
        return (query_grad, key_accum, value_accum)

    start_grad = jnp.zeros(queries.shape, jnp.float32)
    query_grad, key_accum, value_accum = lax.fori_loop(
        lowest, highest, second_pass, (start_grad, carried[0], carried[1])
    )
    return (query_grad, (key_accum, value_accum))


def body(layer_input, query_weight, key_weight, value_weight, out_grad, doc_ids):
    tok_rows = layer_input.shape[0]
    query_width = query_weight.shape[1]
    pair_width = key_weight.shape[1]
    key_heads = pair_width // DH
    group_size = HQ // HK
    block_count = tok_rows // BLOCK
    owner_id = lax.axis_index("srv")
    weights_all = lax.all_gather(
        jnp.concatenate([query_weight, key_weight, value_weight], axis=1), "srv", axis=0, tiled=True
    )
    inputs_all = lax.all_gather(layer_input, ("hid", "rep"), axis=1, tiled=True)
    projected = jnp.dot(inputs_all, weights_all, preferred_element_type=jnp.float32).astype(
        jnp.bfloat16
    )
    queries = projected[:, :query_width].reshape(block_count, BLOCK, key_heads, group_size, DH)
    keys_local = projected[:, query_width : query_width + pair_width]
    values_local = projected[:, query_width + pair_width :]
    keys_all, values_all = (
        lax.all_gather(keys_local, "srv", axis=0, tiled=True),
        lax.all_gather(values_local, "srv", axis=0, tiled=True),
    )
    total_rows = keys_all.shape[0]
    keys_all = keys_all.reshape(total_rows, key_heads, DH)
    values_all = values_all.reshape(total_rows, key_heads, DH)
    cotangent = out_grad.reshape(block_count, BLOCK, key_heads, group_size, DH)
    empty_accum = jnp.zeros((total_rows, key_heads, DH), jnp.float32)

    def own_block(position, loop_state):
        answers, carried = loop_state
        grad_q, carried = attend(
            lax.dynamic_index_in_dim(queries, position, 0, keepdims=False),
            lax.dynamic_index_in_dim(cotangent, position, 0, keepdims=False),
            keys_all,
            values_all,
            doc_ids,
            owner_id * block_count + position,
            carried,
        )
        answers = lax.dynamic_update_index_in_dim(answers, grad_q.astype(jnp.bfloat16), position, 0)
        return (answers, carried)

    answers = jnp.zeros(queries.shape, jnp.bfloat16)
    answers, carried = lax.fori_loop(
        0, block_count, own_block, (answers, (empty_accum, empty_accum))
    )
    query_grad = answers.reshape(tok_rows, query_width)
    key_accum, value_accum = carried
    key_sum, value_sum = (
        lax.psum_scatter(key_accum, "srv", scatter_dimension=0, tiled=True),
        lax.psum_scatter(value_accum, "srv", scatter_dimension=0, tiled=True),
    )
    grads_all = jnp.concatenate(
        [
            query_grad,
            key_sum.astype(jnp.bfloat16).reshape(tok_rows, pair_width),
            value_sum.astype(jnp.bfloat16).reshape(tok_rows, pair_width),
        ],
        axis=1,
    )
    input_terms = lax.dot_general(
        grads_all, weights_all, (((1,), (1,)), ((), ())), preferred_element_type=jnp.float32
    )
    input_grad = lax.psum_scatter(
        input_terms, ("hid", "rep"), scatter_dimension=1, tiled=True
    ).astype(jnp.bfloat16)
    columns = lax.all_to_all(inputs_all, "srv", split_axis=1, concat_axis=0, tiled=True)
    weight_grad = lax.dot_general(
        columns,
        lax.all_gather(grads_all, "srv", axis=0, tiled=True),
        (((0,), (0,)), ((), ())),
        preferred_element_type=jnp.float32,
    )
    return (
        input_grad,
        weight_grad[:, :query_width],
        weight_grad[:, query_width : query_width + pair_width],
        weight_grad[:, query_width + pair_width :],
    )


MESH = pl.DeviceIdType.MESH
VM = pl.BlockSpec(memory_space=pltpu.VMEM)
VMEM_BYTES = 60 * 1024 * 1024


def place(n_rep):
    return lax.axis_index("srv"), lax.axis_index("hid") * n_rep + lax.axis_index("rep")


def device_at(z, c, n_rep):
    return {"srv": z, "hid": c // n_rep, "rep": c % n_rep}


def greet(n, m, n_rep):
    z, c = place(n_rep)
    barrier = pltpu.get_barrier_semaphore()
    for dz in range(n):
        for dc in range(m):
            if dz or dc:
                pl.semaphore_signal(
                    barrier,
                    inc=1,
                    device_id=device_at((z + dz) % n, (c + dc) % m, n_rep),
                    device_id_type=MESH,
                )
    pl.semaphore_wait(barrier, n * m - 1)


def remote(src, dst, send, recv, device):
    return pltpu.make_async_remote_copy(
        src_ref=src, dst_ref=dst, send_sem=send, recv_sem=recv, device_id=device, device_id_type=MESH
    )


def rows_at(start, size):
    return pl.ds(pl.multiple_of(start, size), size)


def cols_at(start, size):
    return pl.ds(pl.multiple_of(start, DH), size)


def attend_rows(heads, qkv, og_ref, dc_ref, dq_ref, dq_cols, dk, dv, first, row_block, low, width):
    q_cols = heads * DH
    scale = DH ** (-0.5)
    rows = rows_at(first, row_block)
    span = rows_at(low, row_block) if width == row_block else pl.ds(pl.multiple_of(low, row_block), width)
    queries = jnp.concatenate([qkv[rows, h * DH : (h + 1) * DH] for h in range(heads)], axis=0)
    cotangent = jnp.concatenate([og_ref[rows, h * DH : (h + 1) * DH] for h in range(heads)], axis=0)
    keys = qkv[span, q_cols : q_cols + DH]
    values = qkv[span, q_cols + DH : q_cols + 2 * DH]
    row_pos = first + lax.broadcasted_iota(jnp.int32, (row_block, width), 0)
    key_pos = low + lax.broadcasted_iota(jnp.int32, (row_block, width), 1)
    row_doc = jnp.broadcast_to(dc_ref[:, rows].astype(jnp.float32), (row_block, row_block)).T[:, :1]
    kept = (row_doc == dc_ref[:, span].astype(jnp.float32)) & (key_pos <= row_pos)
    bias = jnp.concatenate([jnp.where(kept, 0.0, NEGATIVE)] * heads, axis=0)
    both = (((1,), (1,)), ((), ()))
    logits = lax.dot_general(queries, keys, both, preferred_element_type=jnp.float32) * scale + bias
    weights = jnp.exp(logits - jnp.max(logits, axis=1, keepdims=True))
    attention = weights * (1.0 / jnp.sum(weights, axis=1, keepdims=True))
    slopes = lax.dot_general(cotangent, values, both, preferred_element_type=jnp.float32)
    inner = jnp.sum(attention * slopes, axis=1, keepdims=True)
    score_grad = (attention * (slopes - inner) * scale).astype(jnp.bfloat16)
    down = (((0,), (0,)), ((), ()))
    query_grad = jnp.dot(score_grad, keys, preferred_element_type=jnp.float32).astype(jnp.bfloat16)
    for h in range(heads):
        dq_ref[rows, cols_at(dq_cols + h * DH, DH)] = query_grad[h * row_block : (h + 1) * row_block]
    dk[span, :] += lax.dot_general(score_grad, queries, down, preferred_element_type=jnp.float32)
    dv[span, :] += lax.dot_general(
        attention.astype(jnp.bfloat16), cotangent, down, preferred_element_type=jnp.float32
    )


def chain_kernel(
    n, m, n_rep, rows, longest,
    x_ref, og_ref, qw_in, kw_in, vw_in, dc_in,
    turned_out, dqa_out, kva_out, ig_ref,
    qw_ref, kw_ref, vw_ref, dc_ref, cols_ref, turned, dqa_ref, kva_ref, rs_in, rs_out, og_own, dk, dv, hopped, early, terms, took, paired, done,
    h_send, h_recv, a_send, a_recv, b_send, b_recv, og_send, og_recv, rs_send, rs_recv,
    dq_send, dq_recv, kv_send, kv_recv, r_send, r_recv, e_send, e_recv, out_sem, w_sem,
):
    z, c = place(n_rep)
    tok, feats = x_ref.shape
    total = tok * n
    count = total // rows
    per = tok // rows
    piece = rows // m
    parts = tok // (rows // 2)
    share = rows // 4
    q_side = qw_ref.shape[1] // 2
    heads = q_side // DH
    delay = longest // rows
    lead = 5
    half = z // (n // 2)
    e = z * (1 - half) + (n - 1 - z) * half
    f = n - 1 - e
    inner = z + 1 - 2 * half
    outer = z - 1 + 2 * half
    side_b = half
    side_a = 1 - half
    near_end = (n - 1) * half
    far_end = (n - 1) * (1 - half)
    is_end = e == 0
    not_end = e > 0
    sibling = c + 1 - 2 * (c % 2)
    across = (c + 2) % m
    diagonal = across + 1 - 2 * (across % 2)
    sub = rows // 2
    f32, bf16 = jnp.float32, jnp.bfloat16

    def chunk_rows(j):
        return rows_at(j * rows, rows)

    def hop_copy(u):
        src = x_ref.at[rows_at(u * sub, sub)]
        return remote(src, hopped.at[u // 2], h_send, h_recv.at[u // 2], device_at(z, across, n_rep))

    def input_copy(u, i):
        p = (c // 2) * 2 + i
        plane = across if u % 2 else c
        if u % 2:
            src = hopped.at[u // 2, i * share : (i + 1) * share]
        else:
            src = x_ref.at[rows_at(u * sub + i * share, share)]
        dst = cols_ref.at[rows_at(z * tok + u * sub + i * share, share)]
        copy = remote(
            src, dst, a_send.at[u, i], a_recv.at[z * parts + u], device_at(plane, p, n_rep)
        )
        return (plane == z) & (p == c), src, dst, copy

    def send_input(u):
        for i in range(2):
            own, src, dst, copy = input_copy(u, i)

            @pl.when(own)
            def _():
                pltpu.make_async_copy(src, dst, a_recv.at[z * parts + u]).start()

            @pl.when(jnp.logical_not(own))
            def _():
                copy.start()

    def holds(g):
        return (c // 2 + z // (n // 2) + g) % 2 == 0

    def half_block(g):
        return cols_ref.at[rows_at(g * sub + (c % 2) * share, share)]

    def spread_copy(g, slot):
        block = half_block(g)
        return remote(
            block, block, b_send, b_recv.at[g, slot % 2],
            device_at(z, across if slot == 1 else sibling, n_rep),
        )

    def og_copy(u, s, slot, to):
        src = og_ref.at[rows_at(u * rows, rows), cols_at(s * q_side, q_side)]
        dst = og_own.at[chunk_rows(z * per + u)]
        return src, dst, remote(
            src, dst, og_send.at[u, slot], og_recv.at[z * per + u], device_at(to, c, n_rep)
        )

    def sub_rows(g):
        return rows_at(g * sub, sub)

    def rs_copy(s, g, to):
        return remote(
            rs_out.at[s, sub_rows(g)], rs_in.at[s, sub_rows(g)],
            rs_send.at[s], rs_recv.at[s, g], device_at(to, c, n_rep),
        )

    def dq_copy(s, j, to):
        block = dqa_ref.at[chunk_rows(j), cols_at(s * q_side, q_side)]
        return remote(block, block, dq_send.at[s], dq_recv.at[s, j], device_at(to, c, n_rep))

    def kv_copy(s, j, to):
        block = kva_ref.at[:, chunk_rows(j), cols_at(s * DH, DH)]
        return remote(block, block, kv_send.at[s], kv_recv.at[s, j], device_at(to, c, n_rep))

    def term_rows(j, owner):
        return rows_at(j * rows + owner * piece, piece)

    def term_copy(j, slot):
        return remote(
            terms.at[term_rows(j, diagonal if slot else sibling)],
            took.at[slot, rows_at(j * piece, piece)],
            r_send.at[0], r_recv.at[j, slot], device_at(z, sibling, n_rep),
        )

    def pair_copy(j):
        block = rows_at(j * piece, piece)
        return remote(
            paired.at[block], took.at[2, block],
            r_send.at[1], r_recv.at[j, 2], device_at(z, across, n_rep),
        )

    def done_place(j):
        return ig_ref.at[rows_at((j % per) * rows + c * piece, piece)]

    def done_copy(j):
        return remote(
            done.at[rows_at(j * piece, piece)], done_place(j),
            e_send.at[j], e_recv.at[c, j % per], device_at(j // per, z, n_rep),
        )

    def spread(g):
        @pl.when(holds(g))
        def _():
            block = half_block(g)
            pltpu.make_async_copy(block, block, a_recv.at[g]).wait()
            for slot in (1, 0):
                spread_copy(g, slot).start()

    def relay(g):
        @pl.when(jnp.logical_not(holds(g)))
        def _():
            spread_copy(g, 1).wait_recv()
            spread_copy(g, 2).start()

    def await_input(g):
        @pl.when(holds(g))
        def _():
            spread_copy(g, 0).wait_recv()

        @pl.when(jnp.logical_not(holds(g)))
        def _():
            spread_copy(g, 2).wait_recv()

    def project(s, g):
        x = cols_ref[sub_rows(g), :]
        return jnp.concatenate(
            [
                jnp.dot(x, qw_ref[:, cols_at(s * q_side, q_side)], preferred_element_type=f32),
                jnp.dot(x, kw_ref[:, cols_at(s * DH, DH)], preferred_element_type=f32),
                jnp.dot(x, vw_ref[:, cols_at(s * DH, DH)], preferred_element_type=f32),
            ],
            axis=1,
        )

    def add_in(s, g):
        part = project(s, g)
        rs_copy(s, g, inner).wait_recv()
        rs_out[s, sub_rows(g), :] = (part + rs_in[s, sub_rows(g), :].astype(f32)).astype(bf16)

    def out_copy(j, slot):
        if slot == 2:
            src, dst = kva_ref.at[:, chunk_rows(j)], kva_out.at[:, chunk_rows(j)]
        elif slot == 1:
            src, dst = dqa_ref.at[chunk_rows(j)], dqa_out.at[chunk_rows(j)]
        else:
            src, dst = turned.at[:, chunk_rows(j)], turned_out.at[:, chunk_rows(j)]
        return pltpu.make_async_copy(src, dst, out_sem.at[slot])

    def reduce_a(g):
        await_input(g)

        @pl.when(is_end)
        def _():
            rs_out[side_a, sub_rows(g), :] = project(side_a, g).astype(bf16)

        @pl.when(not_end)
        def _():
            add_in(side_a, g)

        rs_copy(side_a, g, inner).start()

    def reduce_b(g):
        add_in(side_b, g)

        @pl.when(not_end)
        def _():
            rs_copy(side_b, g, outer).start()

    def settle(i):
        kva_ref[0, chunk_rows(i), cols_at(side_b * DH, DH)] = dk[chunk_rows(i), :].astype(bf16)
        kva_ref[1, chunk_rows(i), cols_at(side_b * DH, DH)] = dv[chunk_rows(i), :].astype(bf16)
        kv_copy(side_b, i, inner).start()

    def attend_chunk(j):
        block = og_own.at[chunk_rows(j)]
        pltpu.make_async_copy(block, block, og_recv.at[j]).wait()
        run = functools.partial(
            attend_rows, heads, rs_out.at[side_b], og_own, dc_ref, dqa_ref, side_b * q_side, dk, dv
        )
        for b in range(delay):
            @pl.when(j == b)
            def _():
                run(b * rows, rows, 0, (b + 1) * rows)

        @pl.when(j >= delay)
        def _():
            run(j * rows, rows, (j - delay) * rows, (delay + 1) * rows)

        dq_copy(side_b, j, inner).start()

        @pl.when(j >= delay)
        def _():
            settle(j - delay)

        @pl.when(j == count - 1)
        def _():
            def rest(i, carry):
                settle(i)
                return carry

            lax.fori_loop(count - delay, count, rest, 0)

    def combine(j):
        term_copy(j, 1).wait_recv()
        block = rows_at(j * piece, piece)
        value = terms[term_rows(j, across), :].astype(f32) + took[1, block, :].astype(f32)
        paired[block, :] = value.astype(bf16)
        pair_copy(j).start()

    def finish(j):
        block = rows_at(j * piece, piece)
        term_copy(j, 0).wait_recv()
        value = terms[term_rows(j, c), :].astype(f32) + took[0, block, :].astype(f32)
        pair_copy(j).wait_recv()
        value = value + took[2, block, :].astype(f32)
        done[rows_at(j * piece, piece), :] = value.astype(bf16)
        own = (j // per == z) & (c == z)

        @pl.when(own)
        def _():
            pltpu.make_async_copy(
                done.at[rows_at(j * piece, piece)], done_place(j), e_recv.at[c, j % per]
            ).start()

        @pl.when(jnp.logical_not(own))
        def _():
            done_copy(j).start()

    def term(j):
        for slot in (1, 2):
            out_copy(j, slot).start()
        flip = (((1,), (1,)), ((), ()))
        value = early[chunk_rows(j), :]
        value = value + lax.dot_general(
            kva_ref[0, chunk_rows(j), :], kw_ref[...], flip, preferred_element_type=f32
        )
        value = value + lax.dot_general(
            kva_ref[1, chunk_rows(j), :], vw_ref[...], flip, preferred_element_type=f32
        )
        terms[chunk_rows(j), :] = value.astype(bf16)
        for slot in (1, 0):
            term_copy(j, slot).start()

        @pl.when(j > 0)
        def _():
            combine(j - 1)

    def pass_b(v):
        @pl.when(v < count)
        def _():
            dq_copy(side_b, v, inner).wait_recv()
            dq_copy(side_b, v, inner).start()

        @pl.when(v >= delay)
        def _():
            kv_copy(side_b, v - delay, inner).wait_recv()
            kv_copy(side_b, v - delay, inner).start()

    def pass_a(v):
        @pl.when(v < count)
        def _():
            dq_copy(side_a, v, inner).wait_recv()

            @pl.when(not_end)
            def _():
                dq_copy(side_a, v, outer).start()

            early[chunk_rows(v), :] = lax.dot_general(
                dqa_ref[chunk_rows(v), :], qw_ref[...], (((1,), (1,)), ((), ())),
                preferred_element_type=f32,
            )

        @pl.when(v >= delay)
        def _():
            kv_copy(side_a, v - delay, inner).wait_recv()

            @pl.when(not_end)
            def _():
                kv_copy(side_a, v - delay, outer).start()

            term(v - delay)

    loads = [
        pltpu.make_async_copy(qw_in, qw_ref, w_sem.at[0]),
        pltpu.make_async_copy(kw_in, kw_ref, w_sem.at[1]),
        pltpu.make_async_copy(vw_in, vw_ref, w_sem.at[2]),
        pltpu.make_async_copy(dc_in, dc_ref, w_sem.at[3]),
    ]
    for copy in loads:
        copy.start()
    greet(n, m, n_rep)
    send_input(0)
    @pl.when(is_end)
    def _():
        dk[...] = jnp.zeros_like(dk)
        dv[...] = jnp.zeros_like(dv)

    def forward(u):
        hop_copy(u).wait_recv()
        send_input(u)

    def send_og(u, slot):
        to = (far_end, near_end)[slot]
        src, dst, copy = og_copy(u, (side_a, side_b)[slot], slot, to)
        if slot == 0:
            copy.start()
        else:
            @pl.when(is_end)
            def _():
                pltpu.make_async_copy(src, dst, og_recv.at[z * per + u]).start()

            @pl.when(not_end)
            def _():
                copy.start()

    def begin():
        for u in range(1, lead):
            if u < parts and u % 2:
                forward(u)
            spread(u)
        relay(1)
        for u in range(per):
            send_og(u, 1)

            send_og(u, 0)

    spread(0)
    for u in range(1, parts, 2):
        hop_copy(u).start()
    for u in range(2, parts, 2):
        send_input(u)
    for copy in loads:
        copy.wait()
    relay(0)

    def step(k, carry):
        even = k % 2 == 0
        j = k // 2


        @pl.when((k > 0) & (k + 1 < 2 * count))
        def _():
            relay(k + 1)

        @pl.when((k >= 2 * e) & (k < 2 * e + 2 * count))
        def _():
            reduce_a(k - 2 * e)

        @pl.when(k == 0)
        def _():
            begin()

        @pl.when(k + lead < 2 * count)
        def _():
            spread(k + lead)

        @pl.when((k % 2 == 1) & (k >= 2 * e) & (k < 2 * e + 2 * count))
        def _():
            turned[:, chunk_rows(j - e)] = cols_ref[chunk_rows(j - e), :].T
            out_copy(j - e, 0).start()

        @pl.when((k >= 2 * f) & (k < 2 * f + 2 * count))
        def _():
            reduce_b(k - 2 * f)

        h = j + 1

        @pl.when(is_end & (k % 2 == 1) & (h >= n) & (h < n + count))
        def _():
            attend_chunk(h - n)

        @pl.when(not_end & (k % 2 == 1) & (h >= n + e) & (h < n + e + count + delay))
        def _():
            pass_b(h - n - e)

        @pl.when((k % 2 == 1) & (h >= n + f) & (h < n + f + count + delay))
        def _():
            pass_a(h - n - f)

        return carry

    lax.fori_loop(0, 2 * (count + delay + 2 * (n - 1) + 1), step, 0)
    for j in (count - 1,):
        combine(jnp.int32(j))

    def close(j, carry):
        finish(j)
        return carry

    lax.fori_loop(0, count, close, 0)

    def settled(ref, sem):
        pltpu.make_async_copy(ref, ref, sem).wait()

    def drain(j, carry):
        @pl.when(jnp.logical_not((j // per == z) & (c == z)))
        def _():
            done_copy(j).wait_send()

        return carry

    settled(cols_ref.at[: 3 * total // m], b_send)
    settled(terms.at[: 2 * total // m], r_send.at[0])
    settled(paired, r_send.at[1])
    settled(turned, out_sem.at[0])
    settled(dqa_ref, out_sem.at[1])
    settled(kva_ref, out_sem.at[2])
    settled(rs_out.at[side_a], rs_send.at[side_a])
    settled(og_own, dq_send.at[side_b])
    settled(kva_ref.at[side_b], kv_send.at[side_b])

    @pl.when(not_end)
    def _():
        settled(rs_out.at[side_b], rs_send.at[side_b])
        settled(og_own, dq_send.at[side_a])
        settled(kva_ref.at[side_a], kv_send.at[side_a])

    lax.fori_loop(0, count, drain, 0)
    settled(hopped, h_send)
    for u in range(parts):
        for i in range(2):
            own, _, _, copy = input_copy(u, i)

            @pl.when(jnp.logical_not(own))
            def _():
                copy.wait_send()
    for u in range(per):
        _, _, copy = og_copy(u, side_a, 0, far_end)
        copy.wait_send()

        @pl.when(not_end)
        def _():
            _, _, copy = og_copy(u, side_b, 1, near_end)
            copy.wait_send()

        for q in range(m):
            block = ig_ref.at[u * rows + q * piece : u * rows + (q + 1) * piece]
            pltpu.make_async_copy(block, block, e_recv.at[q, u]).wait()


def chained(n, n_hid, n_rep, layer_input, query_weight, key_weight, value_weight, out_grad, doc_ids):
    m = n_hid * n_rep
    bf16, f32 = jnp.bfloat16, jnp.float32
    tok, feats = layer_input.shape
    total = tok * n
    rows = BLOCK
    count, per, piece = total // rows, tok // rows, rows // m
    q_cols = query_weight.shape[1]
    pair_width = key_weight.shape[1]
    width = q_cols // 2 + pair_width
    dma = pltpu.SemaphoreType.DMA
    ANY = pl.BlockSpec(memory_space=pl.ANY)
    HBM = pl.BlockSpec(memory_space=pltpu.HBM)
    held = [
        pltpu.with_memory_space_constraint(array, pltpu.HBM)
        for array in (
            layer_input, out_grad, query_weight, key_weight, value_weight, doc_ids.reshape(1, total)
        )
    ]
    turned, queries_all, pairs_all, input_grad = pl.pallas_call(
        functools.partial(chain_kernel, n, m, n_rep, rows, total // 2),
        out_shape=(
            jax.ShapeDtypeStruct((feats, total), bf16),
            jax.ShapeDtypeStruct((total, q_cols), bf16),
            jax.ShapeDtypeStruct((2, total, pair_width), bf16),
            jax.ShapeDtypeStruct((tok, feats), bf16),
        ),
        in_specs=[HBM] * 6,
        out_specs=(ANY,) * 4,
        scratch_shapes=[
            pltpu.VMEM(query_weight.shape, bf16),
            pltpu.VMEM(key_weight.shape, bf16),
            pltpu.VMEM(value_weight.shape, bf16),
            pltpu.VMEM((1, total), jnp.int32),
            pltpu.VMEM((total, feats), bf16),
            pltpu.VMEM((feats, total), bf16),
            pltpu.VMEM((total, q_cols), bf16),
            pltpu.VMEM((2, total, pair_width), bf16),
            pltpu.VMEM((2, total, width), bf16),
            pltpu.VMEM((2, total, width), bf16),
            pltpu.VMEM((total, q_cols // 2), bf16),
            pltpu.VMEM((total, DH), f32),
            pltpu.VMEM((total, DH), f32),
            pltpu.VMEM((per, rows // 2, feats), bf16),
            pltpu.VMEM((total, feats), f32),
            pltpu.VMEM((total, feats), bf16),
            pltpu.VMEM((3, count * piece, feats), bf16),
            pltpu.VMEM((count * piece, feats), bf16),
            pltpu.VMEM((count * piece, feats), bf16),
            dma, dma((per,)), dma((2 * per, 2)), dma((2 * count,)),
            dma, dma((2 * count, 2)),
            dma((per, 2)), dma((count,)), dma((2,)), dma((2, 2 * count)),
            dma((2,)), dma((2, count)), dma((2,)), dma((2, count)),
            dma((2,)), dma((count, 3)), dma((count,)), dma((m, per)), dma((3,)), dma((4,)),
        ],
        compiler_params=pltpu.CompilerParams(
            collective_id=0, has_side_effects=True, vmem_limit_bytes=44 * 1024 * 1024
        ),
    )(
        *held
    )

    blocks = n
    weight_grads = pl.pallas_call(
        functools.partial(grad_kernel, blocks),
        out_shape=(
            jax.ShapeDtypeStruct((tok, feats), bf16),
            jax.ShapeDtypeStruct((feats, q_cols), f32),
            jax.ShapeDtypeStruct((feats, pair_width), f32),
            jax.ShapeDtypeStruct((feats, pair_width), f32),
        ),
        in_specs=[VM] * 4,
        out_specs=(HBM,) * 4,
        scratch_shapes=[
            pltpu.VMEM((feats, q_cols), f32),
            pltpu.VMEM((feats, pair_width), f32),
            pltpu.VMEM((feats, pair_width), f32),
            dma((blocks, 3)), dma,
        ],
        compiler_params=pltpu.CompilerParams(vmem_limit_bytes=32 * 1024 * 1024),
    )
    return weight_grads(turned, queries_all, pairs_all, input_grad)


def grad_kernel(
    blocks, xt_ref, dq_ref, kv_ref, in_ref, ig_out, qg_out, kg_out, vg_out, qg, kg, vg, sems, sem
):
    whole = pltpu.make_async_copy(in_ref, ig_out, sem)
    whole.start()
    copies = []
    step = xt_ref.shape[0] // blocks
    for b in range(blocks):
        rows = slice(b * step, (b + 1) * step)
        x = xt_ref[rows, :]
        for i, (grads, held, out) in enumerate(
            ((dq_ref, qg, qg_out), (kv_ref.at[0], kg, kg_out), (kv_ref.at[1], vg, vg_out))
        ):
            held[rows, :] = jnp.dot(x, grads[...], preferred_element_type=jnp.float32)
            copy = pltpu.make_async_copy(held.at[rows], out.at[rows], sems.at[b, i])
            copy.start()
            copies.append(copy)
    for copy in copies:
        copy.wait()
    whole.wait()


def solution(mesh):
    in_specs = (
        P(("groups", "srv"), ("hid", "rep")),
        P("srv", ("hid", "rep")),
        P("srv", ("hid", "rep")),
        P("srv", ("hid", "rep")),
        P(("groups", "srv"), ("hid", "rep")),
        P("groups"),
    )
    out_specs = (
        P(("groups", "srv"), ("hid", "rep")),
        P(("groups", "srv"), ("hid", "rep")),
        P(("groups", "srv"), ("hid", "rep")),
        P(("groups", "srv"), ("hid", "rep")),
    )
    n, n_hid, n_rep = mesh.shape["srv"], mesh.shape["hid"], mesh.shape["rep"]
    m = n_hid * n_rep
    inner = body
    if n == m and n_hid == 2 and n_rep == 2 and HK == 2 * m and HQ % HK == 0:
        inner = functools.partial(chained, n, n_hid, n_rep)
    return jax.shard_map(inner, mesh=mesh, in_specs=in_specs, out_specs=out_specs, check_vma=False)
```

```python
import functools

import jax
import jax.numpy as jnp
from jax import lax
from jax.experimental import pallas as pl
from jax.experimental.pallas import tpu as pltpu
from jax.sharding import PartitionSpec as P

HQ = 32
HK = 8
DH = 128
BLOCK = 128


NEGATIVE = -1e30


def attend(queries, cotangent, keys_all, values_all, doc_ids, block_id, carried):
    row_count = queries.shape[0]
    factor_scale = queries.shape[-1] ** (-0.5)
    offsets = jnp.arange(row_count, dtype=jnp.int32)
    query_pos = block_id * row_count + offsets
    query_doc = lax.dynamic_slice_in_dim(doc_ids, block_id * row_count, row_count)
    doc_start = jnp.sum((doc_ids < query_doc[0]).astype(jnp.int32))
    lowest = doc_start // row_count
    highest = jnp.where(True, block_id + 1, lowest)

    def scores_at(key_block):
        key_rows = lax.dynamic_slice_in_dim(keys_all, key_block * row_count, row_count, 0)
        value_rows = lax.dynamic_slice_in_dim(values_all, key_block * row_count, row_count, 0)
        key_doc = lax.dynamic_slice_in_dim(doc_ids, key_block * row_count, row_count)
        key_pos = key_block * row_count + offsets
        allowed = (key_doc[None, :] == query_doc[:, None]) & (
            key_pos[None, :] <= query_pos[:, None]
        )
        logits = (
            jnp.einsum("qgnd,kgd->gnqk", queries, key_rows, preferred_element_type=jnp.float32)
            * factor_scale
        )
        logits = jnp.where(allowed, logits, NEGATIVE)
        slopes = jnp.einsum(
            "qgnd,kgd->gnqk", cotangent, value_rows, preferred_element_type=jnp.float32
        )
        return (key_rows, allowed, logits, slopes)

    def first_pass(key_block, loop_state):
        row_peak, row_total, row_inner = loop_state
        key_rows, allowed, logits, slopes = scores_at(key_block)
        new_peak = jnp.maximum(row_peak, jnp.max(logits, axis=-1))
        weights = jnp.where(allowed, jnp.exp(logits - new_peak[..., None]), 0.0)
        factor = jnp.exp(row_peak - new_peak)
        row_total = row_total * factor + jnp.sum(weights, axis=-1)
        row_inner = row_inner * factor + jnp.sum(weights * slopes, axis=-1)
        return (new_peak, row_total, row_inner)

    stat_shape = (queries.shape[1], queries.shape[2], row_count)
    initial = (
        jnp.full(stat_shape, NEGATIVE, jnp.float32),
        jnp.zeros(stat_shape, jnp.float32),
        jnp.zeros(stat_shape, jnp.float32),
    )
    row_peak, row_total, row_inner = lax.fori_loop(lowest, highest, first_pass, initial)
    safe_total = jnp.where(True, row_total, 1.0)
    row_delta = row_inner / safe_total
    log_total = row_peak + jnp.log(safe_total)

    def second_pass(key_block, loop_state):
        query_grad, key_accum, value_accum = loop_state
        key_rows, allowed, logits, slopes = scores_at(key_block)
        attention = jnp.where(allowed, jnp.exp(logits - log_total[..., None]), 0.0)
        score_grad = (attention * (slopes - row_delta[..., None]) * factor_scale).astype(
            jnp.bfloat16
        )
        value_part = jnp.einsum(
            "gnqk,qgnd->kgd",
            attention.astype(jnp.bfloat16),
            cotangent,
            preferred_element_type=jnp.float32,
        )
        key_part = jnp.einsum(
            "gnqk,qgnd->kgd", score_grad, queries, preferred_element_type=jnp.float32
        )
        query_grad = query_grad + jnp.einsum(
            "gnqk,kgd->qgnd", score_grad, key_rows, preferred_element_type=jnp.float32
        )
        first_row = key_block * row_count
        key_accum = lax.dynamic_update_slice_in_dim(
            key_accum,
            lax.dynamic_slice_in_dim(key_accum, first_row, row_count, 0) + key_part,
            first_row,
            0,
        )
        value_accum = lax.dynamic_update_slice_in_dim(
            value_accum,
            lax.dynamic_slice_in_dim(value_accum, first_row, row_count, 0) + value_part,
            first_row,
            0,
        )
        return (query_grad, key_accum, value_accum)

    start_grad = jnp.zeros(queries.shape, jnp.float32)
    query_grad, key_accum, value_accum = lax.fori_loop(
        lowest, highest, second_pass, (start_grad, carried[0], carried[1])
    )
    return (query_grad, (key_accum, value_accum))


def body(layer_input, query_weight, key_weight, value_weight, out_grad, doc_ids):
    tok_rows = layer_input.shape[0]
    query_width = query_weight.shape[1]
    pair_width = key_weight.shape[1]
    key_heads = pair_width // DH
    group_size = HQ // HK
    block_count = tok_rows // BLOCK
    owner_id = lax.axis_index("srv")
    weights_all = lax.all_gather(
        jnp.concatenate([query_weight, key_weight, value_weight], axis=1), "srv", axis=0, tiled=True
    )
    inputs_all = lax.all_gather(layer_input, ("hid", "rep"), axis=1, tiled=True)
    projected = jnp.dot(inputs_all, weights_all, preferred_element_type=jnp.float32).astype(
        jnp.bfloat16
    )
    queries = projected[:, :query_width].reshape(block_count, BLOCK, key_heads, group_size, DH)
    keys_local = projected[:, query_width : query_width + pair_width]
    values_local = projected[:, query_width + pair_width :]
    keys_all, values_all = (
        lax.all_gather(keys_local, "srv", axis=0, tiled=True),
        lax.all_gather(values_local, "srv", axis=0, tiled=True),
    )
    total_rows = keys_all.shape[0]
    keys_all = keys_all.reshape(total_rows, key_heads, DH)
    values_all = values_all.reshape(total_rows, key_heads, DH)
    cotangent = out_grad.reshape(block_count, BLOCK, key_heads, group_size, DH)
    empty_accum = jnp.zeros((total_rows, key_heads, DH), jnp.float32)

    def own_block(position, loop_state):
        answers, carried = loop_state
        grad_q, carried = attend(
            lax.dynamic_index_in_dim(queries, position, 0, keepdims=False),
            lax.dynamic_index_in_dim(cotangent, position, 0, keepdims=False),
            keys_all,
            values_all,
            doc_ids,
            owner_id * block_count + position,
            carried,
        )
        answers = lax.dynamic_update_index_in_dim(answers, grad_q.astype(jnp.bfloat16), position, 0)
        return (answers, carried)

    answers = jnp.zeros(queries.shape, jnp.bfloat16)
    answers, carried = lax.fori_loop(
        0, block_count, own_block, (answers, (empty_accum, empty_accum))
    )
    query_grad = answers.reshape(tok_rows, query_width)
    key_accum, value_accum = carried
    key_sum, value_sum = (
        lax.psum_scatter(key_accum, "srv", scatter_dimension=0, tiled=True),
        lax.psum_scatter(value_accum, "srv", scatter_dimension=0, tiled=True),
    )
    grads_all = jnp.concatenate(
        [
            query_grad,
            key_sum.astype(jnp.bfloat16).reshape(tok_rows, pair_width),
            value_sum.astype(jnp.bfloat16).reshape(tok_rows, pair_width),
        ],
        axis=1,
    )
    input_terms = lax.dot_general(
        grads_all, weights_all, (((1,), (1,)), ((), ())), preferred_element_type=jnp.float32
    )
    input_grad = lax.psum_scatter(
        input_terms, ("hid", "rep"), scatter_dimension=1, tiled=True
    ).astype(jnp.bfloat16)
    columns = lax.all_to_all(inputs_all, "srv", split_axis=1, concat_axis=0, tiled=True)
    weight_grad = lax.dot_general(
        columns,
        lax.all_gather(grads_all, "srv", axis=0, tiled=True),
        (((0,), (0,)), ((), ())),
        preferred_element_type=jnp.float32,
    )
    return (
        input_grad,
        weight_grad[:, :query_width],
        weight_grad[:, query_width : query_width + pair_width],
        weight_grad[:, query_width + pair_width :],
    )


MESH = pl.DeviceIdType.MESH
VM = pl.BlockSpec(memory_space=pltpu.VMEM)
VMEM_BYTES = 60 * 1024 * 1024


def place(n_rep):
    return lax.axis_index("srv"), lax.axis_index("hid") * n_rep + lax.axis_index("rep")


def device_at(z, c, n_rep):
    return {"srv": z, "hid": c // n_rep, "rep": c % n_rep}


def greet(n, m, n_rep):
    z, c = place(n_rep)
    barrier = pltpu.get_barrier_semaphore()
    for dz in range(n):
        for dc in range(m):
            if dz or dc:
                pl.semaphore_signal(
                    barrier,
                    inc=1,
                    device_id=device_at((z + dz) % n, (c + dc) % m, n_rep),
                    device_id_type=MESH,
                )
    pl.semaphore_wait(barrier, n * m - 1)


def remote(src, dst, send, recv, device):
    return pltpu.make_async_remote_copy(
        src_ref=src, dst_ref=dst, send_sem=send, recv_sem=recv, device_id=device, device_id_type=MESH
    )


def rows_at(start, size):
    return pl.ds(pl.multiple_of(start, size), size)


def cols_at(start, size):
    return pl.ds(pl.multiple_of(start, DH), size)


def attend_rows(heads, qkv, og_ref, dc_ref, dq_ref, dq_cols, dk, dv, first, row_block, low, width):
    q_cols = heads * DH
    scale = DH ** (-0.5)
    rows = rows_at(first, row_block)
    span = rows_at(low, row_block) if width == row_block else pl.ds(pl.multiple_of(low, row_block), width)
    queries = jnp.concatenate([qkv[rows, h * DH : (h + 1) * DH] for h in range(heads)], axis=0)
    cotangent = jnp.concatenate([og_ref[rows, h * DH : (h + 1) * DH] for h in range(heads)], axis=0)
    keys = qkv[span, q_cols : q_cols + DH]
    values = qkv[span, q_cols + DH : q_cols + 2 * DH]
    row_pos = first + lax.broadcasted_iota(jnp.int32, (row_block, width), 0)
    key_pos = low + lax.broadcasted_iota(jnp.int32, (row_block, width), 1)
    row_doc = jnp.broadcast_to(dc_ref[:, rows].astype(jnp.float32), (row_block, row_block)).T[:, :1]
    kept = (row_doc == dc_ref[:, span].astype(jnp.float32)) & (key_pos <= row_pos)
    bias = jnp.concatenate([jnp.where(kept, 0.0, NEGATIVE)] * heads, axis=0)
    both = (((1,), (1,)), ((), ()))
    logits = lax.dot_general(queries, keys, both, preferred_element_type=jnp.float32) * scale + bias
    weights = jnp.exp(logits - jnp.max(logits, axis=1, keepdims=True))
    attention = weights * (1.0 / jnp.sum(weights, axis=1, keepdims=True))
    slopes = lax.dot_general(cotangent, values, both, preferred_element_type=jnp.float32)
    inner = jnp.sum(attention * slopes, axis=1, keepdims=True)
    score_grad = (attention * (slopes - inner) * scale).astype(jnp.bfloat16)
    down = (((0,), (0,)), ((), ()))
    query_grad = jnp.dot(score_grad, keys, preferred_element_type=jnp.float32).astype(jnp.bfloat16)
    for h in range(heads):
        dq_ref[rows, cols_at(dq_cols + h * DH, DH)] = query_grad[h * row_block : (h + 1) * row_block]
    dk[span, :] += lax.dot_general(score_grad, queries, down, preferred_element_type=jnp.float32)
    dv[span, :] += lax.dot_general(
        attention.astype(jnp.bfloat16), cotangent, down, preferred_element_type=jnp.float32
    )


def chain_kernel(
    n, m, n_rep, rows, longest,
    x_ref, og_ref, qw_in, kw_in, vw_in, dc_in,
    turned_out, dqa_out, kva_out, ig_ref,
    qw_ref, kw_ref, vw_ref, dc_ref, cols_ref, turned, dqa_ref, kva_ref, rs_in, rs_out, og_own, dk, dv, hopped, early, terms, took, paired, done,
    h_send, h_recv, a_send, a_recv, b_send, b_recv, og_send, og_recv, rs_send, rs_recv,
    dq_send, dq_recv, kv_send, kv_recv, r_send, r_recv, e_send, e_recv, out_sem, w_sem,
):
    z, c = place(n_rep)
    tok, feats = x_ref.shape
    total = tok * n
    count = total // rows
    per = tok // rows
    piece = rows // m
    parts = tok // (rows // 2)
    share = rows // 4
    q_side = qw_ref.shape[1] // 2
    heads = q_side // DH
    delay = longest // rows
    lead = 5
    half = z // (n // 2)
    e = z * (1 - half) + (n - 1 - z) * half
    f = n - 1 - e
    inner = z + 1 - 2 * half
    outer = z - 1 + 2 * half
    side_b = half
    side_a = 1 - half
    near_end = (n - 1) * half
    far_end = (n - 1) * (1 - half)
    is_end = e == 0
    not_end = e > 0
    sibling = c + 1 - 2 * (c % 2)
    across = (c + 2) % m
    diagonal = across + 1 - 2 * (across % 2)
    sub = rows // 2
    f32, bf16 = jnp.float32, jnp.bfloat16

    def chunk_rows(j):
        return rows_at(j * rows, rows)

    def hop_copy(u):
        src = x_ref.at[rows_at(u * sub, sub)]
        return remote(src, hopped.at[u // 2], h_send, h_recv.at[u // 2], device_at(z, across, n_rep))

    def input_copy(u, i):
        p = (c // 2) * 2 + i
        plane = across if u % 2 else c
        if u % 2:
            src = hopped.at[u // 2, i * share : (i + 1) * share]
        else:
            src = x_ref.at[rows_at(u * sub + i * share, share)]
        dst = cols_ref.at[rows_at(z * tok + u * sub + i * share, share)]
        copy = remote(
            src, dst, a_send.at[u, i], a_recv.at[(z * parts + u) // 2], device_at(plane, p, n_rep)
        )
        return (plane == z) & (p == c), src, dst, copy

    def send_input(u):
        for i in range(2):
            own, src, dst, copy = input_copy(u, i)

            @pl.when(own)
            def _():
                pltpu.make_async_copy(src, dst, a_recv.at[(z * parts + u) // 2]).start()

            @pl.when(jnp.logical_not(own))
            def _():
                copy.start()

    def holds(g):
        return (c // 2 + z // (n // 2) + g) % 2 == 0

    def half_block(g):
        return cols_ref.at[rows_at(g * sub + (c % 2) * share, share)]

    def spread_copy(g, slot):
        block = half_block(g)
        return remote(
            block, block, b_send, b_recv.at[g, slot % 2],
            device_at(z, across if slot == 1 else sibling, n_rep),
        )

    def og_copy(u, s, slot, to):
        src = og_ref.at[rows_at(u * rows, rows), cols_at(s * q_side, q_side)]
        dst = og_own.at[chunk_rows(z * per + u)]
        return src, dst, remote(
            src, dst, og_send.at[u, slot], og_recv.at[z * per + u], device_at(to, c, n_rep)
        )

    def sub_rows(g):
        return rows_at(g * sub, sub)

    def rs_copy(s, g, to):
        return remote(
            rs_out.at[s, sub_rows(g)], rs_in.at[s, sub_rows(g)],
            rs_send.at[s], rs_recv.at[s, g], device_at(to, c, n_rep),
        )

    def dq_copy(s, j, to):
        block = dqa_ref.at[chunk_rows(j), cols_at(s * q_side, q_side)]
        return remote(block, block, dq_send.at[s], dq_recv.at[s, j], device_at(to, c, n_rep))

    def kv_copy(s, j, to):
        block = kva_ref.at[:, chunk_rows(j), cols_at(s * DH, DH)]
        return remote(block, block, kv_send.at[s], kv_recv.at[s, j], device_at(to, c, n_rep))

    def term_rows(j, owner):
        return rows_at(j * rows + owner * piece, piece)

    def term_copy(j, slot):
        return remote(
            terms.at[term_rows(j, diagonal if slot else sibling)],
            took.at[slot, rows_at(j * piece, piece)],
            r_send.at[0], r_recv.at[j, slot], device_at(z, sibling, n_rep),
        )

    def pair_copy(j):
        block = rows_at(j * piece, piece)
        return remote(
            paired.at[block], took.at[2, block],
            r_send.at[1], r_recv.at[j, 2], device_at(z, across, n_rep),
        )

    def done_place(j):
        return ig_ref.at[rows_at((j % per) * rows + c * piece, piece)]

    def done_copy(j):
        return remote(
            done.at[rows_at(j * piece, piece)], done_place(j),
            e_send.at[j], e_recv.at[c, j % per], device_at(j // per, z, n_rep),
        )

    def spread(g):
        @pl.when(holds(g))
        def _():
            block = half_block(g)
            pltpu.make_async_copy(block, block, a_recv.at[g // 2]).wait()
            for slot in (1, 0):
                spread_copy(g, slot).start()

    def relay(g):
        @pl.when(jnp.logical_not(holds(g)))
        def _():
            spread_copy(g, 1).wait_recv()
            spread_copy(g, 2).start()

    def await_input(g):
        @pl.when(holds(g))
        def _():
            spread_copy(g, 0).wait_recv()

        @pl.when(jnp.logical_not(holds(g)))
        def _():
            spread_copy(g, 2).wait_recv()

    def project(s, g):
        x = cols_ref[sub_rows(g), :]
        return jnp.concatenate(
            [
                jnp.dot(x, qw_ref[:, cols_at(s * q_side, q_side)], preferred_element_type=f32),
                jnp.dot(x, kw_ref[:, cols_at(s * DH, DH)], preferred_element_type=f32),
                jnp.dot(x, vw_ref[:, cols_at(s * DH, DH)], preferred_element_type=f32),
            ],
            axis=1,
        )

    def add_in(s, g):
        part = project(s, g)
        rs_copy(s, g, inner).wait_recv()
        rs_out[s, sub_rows(g), :] = (part + rs_in[s, sub_rows(g), :].astype(f32)).astype(bf16)

    def out_copy(j, slot):
        if slot == 2:
            src, dst = kva_ref.at[:, chunk_rows(j)], kva_out.at[:, chunk_rows(j)]
        elif slot == 1:
            src, dst = dqa_ref.at[chunk_rows(j)], dqa_out.at[chunk_rows(j)]
        else:
            src, dst = turned.at[:, chunk_rows(j)], turned_out.at[:, chunk_rows(j)]
        return pltpu.make_async_copy(src, dst, out_sem.at[slot])

    def reduce_a(g):
        await_input(g)

        @pl.when(is_end)
        def _():
            rs_out[side_a, sub_rows(g), :] = project(side_a, g).astype(bf16)

        @pl.when(not_end)
        def _():
            add_in(side_a, g)

        rs_copy(side_a, g, inner).start()

    def reduce_b(g):
        add_in(side_b, g)

        @pl.when(not_end)
        def _():
            rs_copy(side_b, g, outer).start()

    def settle(i):
        kva_ref[0, chunk_rows(i), cols_at(side_b * DH, DH)] = dk[chunk_rows(i), :].astype(bf16)
        kva_ref[1, chunk_rows(i), cols_at(side_b * DH, DH)] = dv[chunk_rows(i), :].astype(bf16)
        kv_copy(side_b, i, inner).start()

    def attend_chunk(j):
        block = og_own.at[chunk_rows(j)]
        pltpu.make_async_copy(block, block, og_recv.at[j]).wait()
        run = functools.partial(
            attend_rows, heads, rs_out.at[side_b], og_own, dc_ref, dqa_ref, side_b * q_side, dk, dv
        )
        for b in range(delay):
            @pl.when(j == b)
            def _():
                run(b * rows, rows, 0, (b + 1) * rows)

        @pl.when(j >= delay)
        def _():
            run(j * rows, rows, (j - delay) * rows, (delay + 1) * rows)

        dq_copy(side_b, j, inner).start()

        @pl.when(j >= delay)
        def _():
            settle(j - delay)

        @pl.when(j == count - 1)
        def _():
            def rest(i, carry):
                settle(i)
                return carry

            lax.fori_loop(count - delay, count, rest, 0)

    def combine(j):
        term_copy(j, 1).wait_recv()
        block = rows_at(j * piece, piece)
        value = terms[term_rows(j, across), :].astype(f32) + took[1, block, :].astype(f32)
        paired[block, :] = value.astype(bf16)
        pair_copy(j).start()

    def finish(j):
        block = rows_at(j * piece, piece)
        term_copy(j, 0).wait_recv()
        value = terms[term_rows(j, c), :].astype(f32) + took[0, block, :].astype(f32)
        pair_copy(j).wait_recv()
        value = value + took[2, block, :].astype(f32)
        done[rows_at(j * piece, piece), :] = value.astype(bf16)
        own = (j // per == z) & (c == z)

        @pl.when(own)
        def _():
            pltpu.make_async_copy(
                done.at[rows_at(j * piece, piece)], done_place(j), e_recv.at[c, j % per]
            ).start()

        @pl.when(jnp.logical_not(own))
        def _():
            done_copy(j).start()

    def term(j):
        for slot in (1, 2):
            out_copy(j, slot).start()
        flip = (((1,), (1,)), ((), ()))
        value = early[chunk_rows(j), :]
        value = value + lax.dot_general(
            kva_ref[0, chunk_rows(j), :], kw_ref[...], flip, preferred_element_type=f32
        )
        value = value + lax.dot_general(
            kva_ref[1, chunk_rows(j), :], vw_ref[...], flip, preferred_element_type=f32
        )
        terms[chunk_rows(j), :] = value.astype(bf16)
        for slot in (1, 0):
            term_copy(j, slot).start()

        @pl.when(j > 0)
        def _():
            combine(j - 1)

    def pass_b(v):
        @pl.when(v < count)
        def _():
            dq_copy(side_b, v, inner).wait_recv()
            dq_copy(side_b, v, inner).start()

        @pl.when(v >= delay)
        def _():
            kv_copy(side_b, v - delay, inner).wait_recv()
            kv_copy(side_b, v - delay, inner).start()

    def pass_a(v):
        @pl.when(v < count)
        def _():
            dq_copy(side_a, v, inner).wait_recv()

            @pl.when(not_end)
            def _():
                dq_copy(side_a, v, outer).start()

            early[chunk_rows(v), :] = lax.dot_general(
                dqa_ref[chunk_rows(v), :], qw_ref[...], (((1,), (1,)), ((), ())),
                preferred_element_type=f32,
            )

        @pl.when(v >= delay)
        def _():
            kv_copy(side_a, v - delay, inner).wait_recv()

            @pl.when(not_end)
            def _():
                kv_copy(side_a, v - delay, outer).start()

            term(v - delay)

    loads = [
        pltpu.make_async_copy(qw_in, qw_ref, w_sem.at[0]),
        pltpu.make_async_copy(kw_in, kw_ref, w_sem.at[1]),
        pltpu.make_async_copy(vw_in, vw_ref, w_sem.at[2]),
        pltpu.make_async_copy(dc_in, dc_ref, w_sem.at[3]),
    ]
    for copy in loads:
        copy.start()
    greet(n, m, n_rep)
    send_input(0)
    @pl.when(is_end)
    def _():
        dk[...] = jnp.zeros_like(dk)
        dv[...] = jnp.zeros_like(dv)

    def forward(u):
        hop_copy(u).wait_recv()
        send_input(u)

    def send_og(u, slot):
        to = (far_end, near_end)[slot]
        src, dst, copy = og_copy(u, (side_a, side_b)[slot], slot, to)
        if slot == 0:
            copy.start()
        else:
            @pl.when(is_end)
            def _():
                pltpu.make_async_copy(src, dst, og_recv.at[z * per + u]).start()

            @pl.when(not_end)
            def _():
                copy.start()

    def begin():
        for u in range(1, lead):
            if u < parts and u % 2:
                forward(u)
            spread(u)
        @pl.when(is_end)
        def _():
            relay(1)

        for u in range(per):
            send_og(u, 0)
        for u in range(per):
            send_og(u, 1)

    spread(0)
    for u in range(1, parts, 2):
        hop_copy(u).start()
    for u in range(2, parts, 2):
        send_input(u)
    for copy in loads:
        copy.wait()
    relay(0)

    def step(k, carry):
        even = k % 2 == 0
        j = k // 2


        @pl.when((k > 0) & (k + 1 - e < 2 * count) & (k + 1 - e > 0))
        def _():
            relay(k + 1 - e)

        @pl.when((k >= 2 * e) & (k < 2 * e + 2 * count))
        def _():
            reduce_a(k - 2 * e)

        @pl.when(k == 0)
        def _():
            begin()

        @pl.when(k + lead < 2 * count)
        def _():
            spread(k + lead)

        @pl.when((k % 2 == 1) & (k >= 2 * e) & (k < 2 * e + 2 * count))
        def _():
            turned[:, chunk_rows(j - e)] = cols_ref[chunk_rows(j - e), :].T
            out_copy(j - e, 0).start()

        @pl.when((k >= 2 * f) & (k < 2 * f + 2 * count))
        def _():
            reduce_b(k - 2 * f)

        h = j + 1

        @pl.when(is_end & (k % 2 == 1) & (h >= n) & (h < n + count))
        def _():
            attend_chunk(h - n)

        @pl.when(not_end & (k % 2 == 1) & (h >= n + e) & (h < n + e + count + delay))
        def _():
            pass_b(h - n - e)

        @pl.when((k % 2 == 1) & (h >= n + f) & (h < n + f + count + delay))
        def _():
            pass_a(h - n - f)

        return carry

    lax.fori_loop(0, 2 * (count + delay + 2 * (n - 1) + 1), step, 0)
    for j in (count - 1,):
        combine(jnp.int32(j))

    def close(j, carry):
        finish(j)
        return carry

    lax.fori_loop(0, count, close, 0)

    def settled(ref, sem):
        pltpu.make_async_copy(ref, ref, sem).wait()

    def drain(j, carry):
        @pl.when(jnp.logical_not((j // per == z) & (c == z)))
        def _():
            done_copy(j).wait_send()

        return carry

    settled(cols_ref.at[: 3 * total // m], b_send)
    settled(terms.at[: 2 * total // m], r_send.at[0])
    settled(paired, r_send.at[1])
    settled(turned, out_sem.at[0])
    settled(dqa_ref, out_sem.at[1])
    settled(kva_ref, out_sem.at[2])
    settled(rs_out.at[side_a], rs_send.at[side_a])
    settled(og_own, dq_send.at[side_b])
    settled(kva_ref.at[side_b], kv_send.at[side_b])

    @pl.when(not_end)
    def _():
        settled(rs_out.at[side_b], rs_send.at[side_b])
        settled(og_own, dq_send.at[side_a])
        settled(kva_ref.at[side_a], kv_send.at[side_a])

    lax.fori_loop(0, count, drain, 0)
    settled(hopped, h_send)
    for u in range(parts):
        for i in range(2):
            own, _, _, copy = input_copy(u, i)

            @pl.when(jnp.logical_not(own))
            def _():
                copy.wait_send()
    for u in range(per):
        _, _, copy = og_copy(u, side_a, 0, far_end)
        copy.wait_send()

        @pl.when(not_end)
        def _():
            _, _, copy = og_copy(u, side_b, 1, near_end)
            copy.wait_send()

        for q in range(m):
            block = ig_ref.at[u * rows + q * piece : u * rows + (q + 1) * piece]
            pltpu.make_async_copy(block, block, e_recv.at[q, u]).wait()


def chained(n, n_hid, n_rep, layer_input, query_weight, key_weight, value_weight, out_grad, doc_ids):
    m = n_hid * n_rep
    bf16, f32 = jnp.bfloat16, jnp.float32
    tok, feats = layer_input.shape
    total = tok * n
    rows = BLOCK
    count, per, piece = total // rows, tok // rows, rows // m
    q_cols = query_weight.shape[1]
    pair_width = key_weight.shape[1]
    width = q_cols // 2 + pair_width
    dma = pltpu.SemaphoreType.DMA
    ANY = pl.BlockSpec(memory_space=pl.ANY)
    HBM = pl.BlockSpec(memory_space=pltpu.HBM)
    held = [
        pltpu.with_memory_space_constraint(array, pltpu.HBM)
        for array in (
            layer_input, out_grad, query_weight, key_weight, value_weight, doc_ids.reshape(1, total)
        )
    ]
    turned, queries_all, pairs_all, input_grad = pl.pallas_call(
        functools.partial(chain_kernel, n, m, n_rep, rows, total // 2),
        out_shape=(
            jax.ShapeDtypeStruct((feats, total), bf16),
            jax.ShapeDtypeStruct((total, q_cols), bf16),
            jax.ShapeDtypeStruct((2, total, pair_width), bf16),
            jax.ShapeDtypeStruct((tok, feats), bf16),
        ),
        in_specs=[HBM] * 6,
        out_specs=(ANY,) * 4,
        scratch_shapes=[
            pltpu.VMEM(query_weight.shape, bf16),
            pltpu.VMEM(key_weight.shape, bf16),
            pltpu.VMEM(value_weight.shape, bf16),
            pltpu.VMEM((1, total), jnp.int32),
            pltpu.VMEM((total, feats), bf16),
            pltpu.VMEM((feats, total), bf16),
            pltpu.VMEM((total, q_cols), bf16),
            pltpu.VMEM((2, total, pair_width), bf16),
            pltpu.VMEM((2, total, width), bf16),
            pltpu.VMEM((2, total, width), bf16),
            pltpu.VMEM((total, q_cols // 2), bf16),
            pltpu.VMEM((total, DH), f32),
            pltpu.VMEM((total, DH), f32),
            pltpu.VMEM((per, rows // 2, feats), bf16),
            pltpu.VMEM((total, feats), f32),
            pltpu.VMEM((total, feats), bf16),
            pltpu.VMEM((3, count * piece, feats), bf16),
            pltpu.VMEM((count * piece, feats), bf16),
            pltpu.VMEM((count * piece, feats), bf16),
            dma, dma((per,)), dma((2 * per, 2)), dma((count,)),
            dma, dma((2 * count, 2)),
            dma((per, 2)), dma((count,)), dma((2,)), dma((2, 2 * count)),
            dma((2,)), dma((2, count)), dma((2,)), dma((2, count)),
            dma((2,)), dma((count, 3)), dma((count,)), dma((m, per)), dma((3,)), dma((4,)),
        ],
        compiler_params=pltpu.CompilerParams(
            collective_id=0, has_side_effects=True, vmem_limit_bytes=44 * 1024 * 1024
        ),
    )(
        *held
    )

    blocks = n
    weight_grads = pl.pallas_call(
        functools.partial(grad_kernel, blocks),
        out_shape=(
            jax.ShapeDtypeStruct((tok, feats), bf16),
            jax.ShapeDtypeStruct((feats, q_cols), f32),
            jax.ShapeDtypeStruct((feats, pair_width), f32),
            jax.ShapeDtypeStruct((feats, pair_width), f32),
        ),
        in_specs=[VM] * 4,
        out_specs=(HBM,) * 4,
        scratch_shapes=[
            pltpu.VMEM((feats, q_cols), f32),
            pltpu.VMEM((feats, pair_width), f32),
            pltpu.VMEM((feats, pair_width), f32),
            dma((blocks, 3)), dma,
        ],
        compiler_params=pltpu.CompilerParams(vmem_limit_bytes=32 * 1024 * 1024),
    )
    return weight_grads(turned, queries_all, pairs_all, input_grad)


def grad_kernel(
    blocks, xt_ref, dq_ref, kv_ref, in_ref, ig_out, qg_out, kg_out, vg_out, qg, kg, vg, sems, sem
):
    whole = pltpu.make_async_copy(in_ref, ig_out, sem)
    whole.start()
    copies = []
    step = xt_ref.shape[0] // blocks
    for b in range(blocks):
        rows = slice(b * step, (b + 1) * step)
        x = xt_ref[rows, :]
        for i, (grads, held, out) in enumerate(
            ((dq_ref, qg, qg_out), (kv_ref.at[0], kg, kg_out), (kv_ref.at[1], vg, vg_out))
        ):
            held[rows, :] = jnp.dot(x, grads[...], preferred_element_type=jnp.float32)
            copy = pltpu.make_async_copy(held.at[rows], out.at[rows], sems.at[b, i])
            copy.start()
            copies.append(copy)
    for copy in copies:
        copy.wait()
    whole.wait()


def solution(mesh):
    in_specs = (
        P(("groups", "srv"), ("hid", "rep")),
        P("srv", ("hid", "rep")),
        P("srv", ("hid", "rep")),
        P("srv", ("hid", "rep")),
        P(("groups", "srv"), ("hid", "rep")),
        P("groups"),
    )
    out_specs = (
        P(("groups", "srv"), ("hid", "rep")),
        P(("groups", "srv"), ("hid", "rep")),
        P(("groups", "srv"), ("hid", "rep")),
        P(("groups", "srv"), ("hid", "rep")),
    )
    n, n_hid, n_rep = mesh.shape["srv"], mesh.shape["hid"], mesh.shape["rep"]
    m = n_hid * n_rep
    inner = body
    if n == m and n_hid == 2 and n_rep == 2 and HK == 2 * m and HQ % HK == 0:
        inner = functools.partial(chained, n, n_hid, n_rep)
    return jax.shard_map(inner, mesh=mesh, in_specs=in_specs, out_specs=out_specs, check_vma=False)
```
